256 devices in a mesh: branch: 4 (over z_lo), row: 4 (over x), col: 16 (over y, z_hi, core).
Axes of the slice: x: 4, y: 4, z: 8 (z_hi: 2, z_lo: 4; z = z_hi * 4 + z_lo), core: 2. Of those that a mesh axis runs over, the one named last changes fastest.
Arguments:
- section_in: bfloat16 [4, 4, 16, 48, 4096], P('branch', 'row', 'col'), may hold values from -6 to 6
- conv_weight: bfloat16 [4, 2, 3, 3, 384, 384], P('branch'), may hold values from -1 to 1, as said below
- conv_bias: float32 [4, 2, 384], P('branch'), may hold values from -3 to 3
- join_weight: bfloat16 [720, 720], replicated, may hold values from -0.4375 to 0.4375
- join_bias: float32 [720], replicated, may hold values from -3 to 3
Outputs:
- joined_first: bfloat16 [48, 128, 2048], P(None, ('branch', 'row'), 'col')
- joined_second: bfloat16 [96, 64, 1024], P(None, ('branch', 'row'), 'col')
- joined_third: bfloat16 [192, 32, 512], P(None, ('branch', 'row'), 'col')
- joined_fourth: bfloat16 [384, 16, 256], P(None, ('branch', 'row'), 'col')
The draws below stay inside these ranges and needn't reach their ends.
Inputs may be any that keep to these rules, and one draw needn't show every extreme that they name: `conv_weight`: entries of branch b's kernels have standard deviation (9 * 2^b * 48) ** -0.5; entries outside the C_b x C_b corner are drawn too and unused.
All inputs are finite; a program needn't handle non-finite values.
Results may differ from the reference program's by a relative error of at most 0.0075.
Values may be sent and summed in bfloat16 or wider, within the bound.
No kernel may reach another device: no remote copies, remote signals or barrier semaphores. Data moves between devices by JAX's collectives and lax.ppermute only.
A program may use at most 128 MiB of HBM per device.

```python
import jax
import jax.numpy as jnp
from jax import lax

WIDTH = 48
TH = 32
TW = 128
N_BRANCH = 4
N_ROW = 4
N_COL = 16


def draw_conv_weight(key, part):
    array_dims = (4, 2, 3, 3, 8 * WIDTH, 8 * WIDTH)
    fan_scale = (9.0 * WIDTH * 2.0 ** jnp.arange(4, dtype=jnp.float32)) ** (-0.5)
    values = jax.random.normal(key, array_dims, jnp.float32)
    values = jnp.clip(values, -6.0, 6.0)
    return (values * fan_scale[:, None, None, None, None, None]).astype(jnp.bfloat16)


def block_scale(rng, shape, pieces, low, largest):
    gain = 1.0
    for position, parts in pieces:
        draws = jax.random.uniform(jax.random.fold_in(jax.random.fold_in(rng, 6), position), (parts,), jnp.float32, low / len(pieces), largest / len(pieces))
        gain = gain * jnp.repeat(jnp.exp(draws), shape[position] // parts).reshape((-1,) + (1,) * (len(shape) - 1 - position))
    return gain


def bell_draw(stream_key, dims, width, limit, split=(), held_as=jnp.bfloat16):
    values = width * jax.random.normal(stream_key, dims, jnp.float32)
    if split:
        values = values * block_scale(stream_key, dims, split, -0.22, 0.18)
    return jnp.clip(values, -limit, limit).astype(held_as)


def setup_inputs(seed: int = 0) -> dict:
    key_list = jax.random.split(jax.random.key(seed), 6)
    section_in = bell_draw(key_list[0], (N_BRANCH, N_ROW, N_COL, WIDTH, TH * TW), 1.0, 6.0, ((0, 4), (1, 4), (2, 16)))
    conv_weight = draw_conv_weight(jax.random.fold_in(key_list[5], 71), 0)
    conv_bias = bell_draw(key_list[2], (N_BRANCH, 2, 8 * WIDTH), 0.5, 3.0, ((0, 4),), jnp.float32)
    join_weight = bell_draw(key_list[3], (15 * WIDTH, 15 * WIDTH), (4 * WIDTH) ** -0.5, 0.4375)
    join_bias = bell_draw(key_list[4], (15 * WIDTH,), 0.5, 3.0, (), jnp.float32)
    return {"section_in": section_in, "conv_weight": conv_weight, "conv_bias": conv_bias, "join_weight": join_weight, "join_bias": join_bias}


def branch_map(section_in, branch_level):
    channels = WIDTH * 2 ** branch_level
    tile_rows = TH // 2 ** branch_level
    tile_cols = TW // 2 ** branch_level
    packed = section_in[branch_level][:, :, :, : (TH * TW) // 2 ** branch_level]
    packed = packed.reshape(N_ROW, N_COL, channels, tile_rows, tile_cols)
    return packed.transpose(2, 0, 3, 1, 4).reshape(channels, N_ROW * tile_rows, N_COL * tile_cols)


def conv_same(field, kernel):
    result = lax.conv_general_dilated(
        field[None].astype(jnp.float32),
        kernel.astype(jnp.float32).transpose(2, 3, 0, 1),
        (1, 1),
        "SAME",
        dimension_numbers=("NCHW", "OIHW", "NCHW"),
        precision=lax.Precision.HIGHEST,
    )
    return result[0]


def pooled(tile_data, factor):
    channels, height, breadth = tile_data.shape
    blocks = tile_data.astype(jnp.float32).reshape(channels, height // factor, factor, breadth // factor, factor)
    return jnp.mean(blocks, axis=(2, 4)).astype(jnp.bfloat16)


def upsample(tile_data, factor):
    channels, height, breadth = tile_data.shape
    spread = jnp.broadcast_to(tile_data[:, :, None, :, None], (channels, height, factor, breadth, factor))
    return spread.reshape(channels, height * factor, breadth * factor)


def mix_block(join_weight, target, source, tile_data):
    target_start = (2 ** target - 1) * WIDTH
    source_start = (2 ** source - 1) * WIDTH
    target_width = WIDTH * 2 ** target
    source_width = WIDTH * 2 ** source
    block = join_weight[target_start:target_start + target_width, source_start:source_start + source_width]
    channels, height, breadth = tile_data.shape
    product = jnp.dot(block, tile_data.reshape(channels, height * breadth), preferred_element_type=jnp.float32)
    return product.astype(jnp.bfloat16).reshape(target_width, height, breadth)


def reference(section_in, conv_weight, conv_bias, join_weight, join_bias):
    settled = []
    for branch_level in range(4):
        channels = WIDTH * 2 ** branch_level
        inputs = branch_map(section_in, branch_level)
        kernel_first = conv_weight[branch_level, 0, :, :, :channels, :channels]
        kernel_second = conv_weight[branch_level, 1, :, :, :channels, :channels]
        hidden = jax.nn.relu(conv_same(inputs, kernel_first) + conv_bias[branch_level, 0, :channels, None, None])
        hidden = hidden.astype(jnp.bfloat16)
        after = conv_same(hidden, kernel_second) + conv_bias[branch_level, 1, :channels, None, None]
        settled.append(jax.nn.relu(after + inputs.astype(jnp.float32)).astype(jnp.bfloat16))
    outputs = []
    for target in range(4):
        target_start = (2 ** target - 1) * WIDTH
        target_width = WIDTH * 2 ** target
        total_sum = settled[target].astype(jnp.float32) + join_bias[target_start:target_start + target_width, None, None]
        for source in range(4):
            if source < target:
                term = mix_block(join_weight, target, source, pooled(settled[source], 2 ** (target - source)))
                total_sum = total_sum + term.astype(jnp.float32)
            elif source > target:
                term = mix_block(join_weight, target, source, settled[source])
                total_sum = total_sum + upsample(term, 2 ** (source - target)).astype(jnp.float32)
        outputs.append(jax.nn.relu(total_sum).astype(jnp.bfloat16))
    return (outputs[0], outputs[1], outputs[2], outputs[3])
```

```python
import jax
import jax.numpy as jnp
from jax import lax
from jax.experimental import pallas as pl
from jax.experimental.pallas import tpu as pltpu
from jax.sharding import PartitionSpec as P

WIDTH = 48
TH = 32
TW = 128
MARGIN = 128
BF = jnp.bfloat16
F32 = jnp.float32
VMEM = pl.BlockSpec(memory_space=pltpu.VMEM)


def up128(n):
    return -(-n // 128) * 128


class Geo:
    def __init__(self, b):
        self.b = b
        self.parts = 1 << b
        self.channels = WIDTH << b
        self.rows = TH >> b
        self.cols = TW >> b
        self.pixels = self.rows * self.cols
        self.pitch = self.cols + 4
        self.high = self.rows + 4
        self.n1 = up128((self.high - 2) * self.pitch)
        self.n2 = up128((self.high - 4) * self.pitch)
        self.width_x = up128(MARGIN + 2 * self.pitch + 1 + self.n1)
        self.width_h = up128(MARGIN + 2 * self.pitch + 1 + self.n2)
        self.start = ((1 << b) - 1) * WIDTH


GEO = [Geo(b) for b in range(4)]


def place():
    return lax.axis_index("branch"), lax.axis_index("row"), lax.axis_index("col")


def per_branch(body):
    branch = place()[0]
    for g in GEO:

        @pl.when(branch == g.b)
        def _(g=g):
            body(g)


def rows_kernel(x, top, bottom):
    def body(g):
        n = 2 * g.cols
        for q in range(g.parts):
            base = q * g.pixels
            top[:, q * n : (q + 1) * n] = x[:, base : base + n]
            bottom[:, q * n : (q + 1) * n] = x[:, base + g.pixels - n : base + g.pixels]

    per_branch(body)


def source_row(g, x, above, below, q, y):
    if y < 2:
        return above, q * 2 * g.cols + y * g.cols
    if y < g.rows + 2:
        return x, q * g.pixels + (y - 2) * g.cols
    return below, q * 2 * g.cols + (y - g.rows - 2) * g.cols


def cols_kernel(x, above, below, west, east):
    def body(g):
        for q in range(g.parts):
            for y in range(g.high):
                ref, lane = source_row(g, x, above, below, q, y)
                at = q * 2 * g.high + 2 * y
                west[:, at : at + 2] = ref[:, lane : lane + 2]
                last = lane + g.cols - 2
                east[:, at : at + 2] = ref[:, last : last + 2]

    per_branch(body)


def channel_order(g):
    out = lax.broadcasted_iota(jnp.int32, (g.channels, g.channels), 0)
    k = lax.broadcasted_iota(jnp.int32, (g.channels, g.channels), 1)
    part = jnp.zeros_like(k)
    for m in range(1, g.parts):
        part = part + (k >= WIDTH * m).astype(jnp.int32)
    at = (k - WIDTH * part) * g.parts + part
    return (at == out).astype(F32).astype(BF)


def inside(g, row_place, col_place):
    p = lax.broadcasted_iota(jnp.int32, (8, g.n1), 1).astype(F32)
    y = jnp.floor((p + 0.5) * (1.0 / g.pitch))
    x = p - y * g.pitch
    y = y + 1.0
    outside = (
        ((y == 1.0) & (row_place == 0))
        | ((y == g.rows + 2.0) & (row_place == 3))
        | ((x == 1.0) & (col_place == 0))
        | ((x == g.cols + 2.0) & (col_place == 15))
    )
    return jnp.where(outside, 0.0, 1.0)[0:1, :]


def block_kernel(x, above, below, left, right, weight, bias, o0, o1, o2, o3, *scratch):
    outs = (o0, o1, o2, o3)
    wbuf, sems, wcat, col, z0 = scratch[:5]
    xs_all = (None,) + scratch[5:8]
    xp_all = scratch[8:12]
    hp_all = scratch[12:16]
    zt_all = (None,) + scratch[16:19]
    _, row_place, col_place = place()

    def body(g):
        c = g.channels
        cl = up128(c)

        def fetch(layer):
            return pltpu.make_async_copy(
                weight.at[0, layer, :, :, 0:c, 0:cl],
                wbuf.at[layer, :, :, 0:c, 0:cl],
                sems.at[layer],
            )

        fetch(0).start()
        fetch(1).start()
        xp, hp = xp_all[g.b], hp_all[g.b]
        xs = xp if g.b == 0 else xs_all[g.b]
        for q in range(g.parts):
            rows = slice(q * WIDTH, (q + 1) * WIDTH)
            for y in range(g.high):
                ref, lane = source_row(g, x, above, below, q, y)
                at = MARGIN + y * g.pitch
                edge = q * 2 * g.high + 2 * y
                xs[rows, at : at + 2] = left[:, edge : edge + 2]
                xs[rows, at + 2 : at + 2 + g.cols] = ref[:, lane : lane + g.cols]
                xs[rows, at + 2 + g.cols : at + g.pitch] = right[:, edge : edge + 2]
        if g.b:
            xp[...] = jnp.dot(channel_order(g), xs[...], preferred_element_type=F32).astype(BF)

        mask = inside(g, row_place, col_place)

        def column(layer):
            wide = jnp.broadcast_to(bias[0, layer : layer + 1, :], (8, 8 * WIDTH))
            return wide.T[0:c, 0:1]

        def taps():
            for dy in range(3):
                for dx in range(3):
                    yield dy, dx, MARGIN + dy * g.pitch + dx - 1

        def conv(layer, source, n, finish):
            fetch(layer).wait()
            if g.b == 0:
                for dy, dx, lane in taps():
                    t = 3 * dy + dx
                    wcat[:, WIDTH * t : WIDTH * (t + 1)] = wbuf[layer, dy, dx, 0:c, 0:c]
                    col[WIDTH * t : WIDTH * (t + 1), 0:n] = source[:, lane : lane + n]
                step = 384
                for at in range(0, n, step):
                    size = min(step, n - at)
                    finish(
                        at,
                        size,
                        jnp.dot(
                            wcat[...], col[:, at : at + size], preferred_element_type=F32
                        ),
                    )
            else:
                total = None
                for dy, dx, lane in taps():
                    term = jnp.dot(
                        wbuf[layer, dy, dx, 0:c, 0:c],
                        source[:, lane : lane + n],
                        preferred_element_type=F32,
                    )
                    total = term if total is None else total + term
                finish(0, n, total)

        bias0 = column(0)

        def finish_first(at, size, total):
            h = jnp.maximum(total + bias0, 0.0) * mask[:, at : at + size]
            hp[:, MARGIN + at : MARGIN + at + size] = h.astype(BF)

        conv(0, xp, g.n1, finish_first)

        bias1 = column(1)

        def finish_second(at, size, total):
            lane = MARGIN + 2 * g.pitch + at
            own = xp[:, lane : lane + size].astype(F32)
            z = jnp.maximum(total + bias1 + own, 0.0)
            if g.b == 0:
                z0[:, at : at + size] = z.astype(BF)
            else:
                zt_all[g.b][...] = z.T

        conv(1, hp, g.n2, finish_second)

        strip = g.rows // 4
        for y in range(g.rows):
            out = outs[(y // strip - g.b) % 4]
            at = y * g.pitch + 2
            if g.b == 0:
                r = (y % strip) * WIDTH
                out[r : r + WIDTH, :] = z0[:, at : at + g.cols]
                continue
            values = zt_all[g.b][at : at + g.cols, :].astype(BF)
            for m in range(cl // 128):
                r = m * strip * g.cols + (y % strip) * g.cols
                lanes = min(128, c - 128 * m)
                out[r : r + g.cols, 0:lanes] = values[:, 128 * m : 128 * m + lanes]

    per_branch(body)


def repeat_map(j, i):
    gj, gi = GEO[j], GEO[i]
    shape = (gj.pixels // 4, gi.pixels // 4)
    fine = lax.broadcasted_iota(jnp.int32, shape, 0)
    coarse = lax.broadcasted_iota(jnp.int32, shape, 1)
    return cover(fine, coarse, gj, i - j)


def cover(fine, coarse, g, d):
    bits = 7 - g.b
    y = fine >> bits
    x = fine & (g.cols - 1)
    return (((y >> d) << (bits - d)) + (x >> d) == coarse).astype(F32).astype(BF)


def repeat_map_t(j, i):
    gj, gi = GEO[j], GEO[i]
    shape = (gi.pixels // 4, gj.pixels // 4)
    coarse = lax.broadcasted_iota(jnp.int32, shape, 0)
    fine = lax.broadcasted_iota(jnp.int32, shape, 1)
    return cover(fine, coarse, gj, i - j)


def nn(a, b):
    return jnp.dot(a, b, preferred_element_type=F32)


def nt(a, b):
    return lax.dot_general(a, b, (((1,), (1,)), ((), ())), preferred_element_type=F32)


def join_kernel(r0, r1, r2, r3, weight, bias, out0, out1, out2, out3, zb, z0s, s0):
    received = (r0, r1, r2, r3)
    row_place = place()[1]
    for g in GEO:
        used = (384, 256, 128, 48)[g.b]
        for j in range(4):

            @pl.when((row_place + 4 - g.b) % 4 == j)
            def _(g=g, j=j, used=used):
                zb[g.b, 0:used, :] = received[j][0:used, :]

    for y in range(8):
        z0s[:, 128 * y : 128 * (y + 1)] = zb[0, WIDTH * y : WIDTH * (y + 1), :]
    z = [
        z0s[...],
        zb[1, 0:256, 0:96],
        jnp.concatenate([zb[2, 0:64, :], zb[2, 64:128, 0:64]], axis=1),
        jnp.concatenate([zb[3, 0:16, :], zb[3, 16:32, :], zb[3, 32:48, :]], axis=1),
    ]

    def block(j, i):
        gj, gi = GEO[j], GEO[i]
        return weight[gj.start : gj.start + gj.channels, gi.start : gi.start + gi.channels]

    total = None
    for i in (1, 2, 3):
        term = nn(nt(block(0, i), z[i]).astype(BF), repeat_map_t(0, i))
        total = term if total is None else total + term
    wide = jnp.broadcast_to(bias[:, 0:WIDTH], (8, WIDTH))
    total = jnp.maximum(total + z[0].astype(F32) + wide.T[:, 0:1], 0.0)
    for y in range(8):
        s0[:, y, :] = total[:, 128 * y : 128 * (y + 1)]
    out0[...] = s0[...].astype(BF)

    for j, out in ((1, out1), (2, out2), (3, out3)):
        g = GEO[j]
        total = z[j].astype(F32) + bias[:, g.start : g.start + g.channels]
        for i in range(4):
            if i == j:
                continue
            if i < j:
                sums = (nt if i == 0 else nn)(repeat_map_t(i, j), z[i])
                mean = (sums * (0.25 ** (j - i))).astype(BF)
                total = total + nt(mean, block(j, i)).astype(BF).astype(F32)
            else:
                total = total + nn(repeat_map(j, i), nt(z[i], block(j, i)).astype(BF))
        out[...] = jnp.maximum(total, 0.0).astype(BF)


def params():
    return pltpu.CompilerParams(vmem_limit_bytes=40 * 1024 * 1024)


def like(*shapes):
    return tuple(jax.ShapeDtypeStruct(s, BF) for s in shapes)


def call_rows(x):
    return pl.pallas_call(
        rows_kernel,
        out_shape=like((WIDTH, 256), (WIDTH, 256)),
        in_specs=[VMEM],
        out_specs=(VMEM, VMEM),
        compiler_params=params(),
    )(x)


def call_cols(x, above, below):
    return pl.pallas_call(
        cols_kernel,
        out_shape=like((WIDTH, 128), (WIDTH, 128)),
        in_specs=[VMEM] * 3,
        out_specs=(VMEM, VMEM),
        compiler_params=params(),
    )(x, above, below)


def call_block(x, above, below, left, right, weight, bias):
    scratch = [
        pltpu.VMEM((2, 3, 3, 384, 384), BF),
        pltpu.SemaphoreType.DMA((2,)),
        pltpu.VMEM((WIDTH, 9 * WIDTH), BF),
        pltpu.VMEM((9 * WIDTH, GEO[0].n1), BF),
        pltpu.VMEM((WIDTH, GEO[0].n2), BF),
    ]
    scratch += [pltpu.VMEM((g.channels, g.width_x), BF) for g in GEO[1:]]
    scratch += [pltpu.VMEM((g.channels, g.width_x), BF) for g in GEO]
    scratch += [pltpu.VMEM((g.channels, g.width_h), BF) for g in GEO]
    scratch += [pltpu.VMEM((g.n2, g.channels), F32) for g in GEO[1:]]
    return pl.pallas_call(
        block_kernel,
        out_shape=like(*[(384, 128)] * 4),
        in_specs=[VMEM] * 5 + [pl.BlockSpec(memory_space=pl.ANY), VMEM],
        out_specs=(VMEM,) * 4,
        scratch_shapes=scratch,
        compiler_params=params(),
    )(x, above, below, left, right, weight, bias)


def call_join(received, weight, bias):
    return pl.pallas_call(
        join_kernel,
        out_shape=like((WIDTH, 8, 128), (256, 96), (64, 192), (16, 384)),
        in_specs=[VMEM] * 6,
        out_specs=(VMEM,) * 4,
        scratch_shapes=[
            pltpu.VMEM((4, 384, 128), BF),
            pltpu.VMEM((WIDTH, 1024), BF),
            pltpu.VMEM((WIDTH, 8, 128), F32),
        ],
        compiler_params=params(),
    )(*received, weight, bias)


def shifted(shard, axis, by):
    size = lax.axis_size(axis)
    pairs = [(i, i + by) for i in range(size) if 0 <= i + by < size]
    return lax.ppermute(shard, axis, pairs)


def exchanged(parts):
    return [
        lax.ppermute(
            part,
            ("branch", "row"),
            [(b * 4 + r, r * 4 + (b + j) % 4) for b in range(4) for r in range(4)],
        )
        for j, part in enumerate(parts)
    ]


def local(section_in, conv_weight, conv_bias, join_weight, join_bias):
    x = section_in[0, 0, 0]
    top, bottom = call_rows(x)
    above = shifted(bottom, "row", 1)
    below = shifted(top, "row", -1)
    west, east = call_cols(x, above, below)
    left = shifted(east, "col", 1)
    right = shifted(west, "col", -1)
    parts = call_block(x, above, below, left, right, conv_weight, conv_bias)
    received = exchanged(parts)
    out = call_join(received, join_weight, join_bias[None, :])
    first = [out[0]]
    for g in GEO[1:]:
        pixel_major = out[g.b].reshape(g.rows // 4, g.cols, g.channels)
        first.append(pixel_major.transpose(2, 0, 1))
    return tuple(first)


def solution(mesh):
    in_specs = (
        P("branch", "row", "col", None, None),
        P("branch", None, None, None, None, None),
        P("branch", None, None),
        P(),
        P(),
    )
    out_specs = (P(None, ("branch", "row"), "col"),) * 4
    return jax.shard_map(local, mesh=mesh, in_specs=in_specs, out_specs=out_specs, check_vma=False)
```

```python
import jax
import jax.numpy as jnp
from jax import lax
from jax.experimental import pallas as pl
from jax.experimental.pallas import tpu as pltpu
from jax.sharding import PartitionSpec as P

WIDTH = 48
TH = 32
TW = 128
MARGIN = 128
BF = jnp.bfloat16
F32 = jnp.float32
VMEM = pl.BlockSpec(memory_space=pltpu.VMEM)


def up128(n):
    return -(-n // 128) * 128


class Geo:
    def __init__(self, b):
        self.b = b
        self.parts = 1 << b
        self.channels = WIDTH << b
        self.rows = TH >> b
        self.cols = TW >> b
        self.pixels = self.rows * self.cols
        self.strip = self.rows // 4
        self.high = self.strip + 4
        self.main = self.high * self.cols
        self.side = self.high * 2
        self.slot = up128(self.main + 2 * self.side)
        self.pitch = self.cols + 4
        self.wide = 4 * self.pitch
        self.n1 = up128((self.strip + 2) * self.wide)
        self.n2 = up128(self.strip * self.wide)
        self.width_x = up128(MARGIN + 2 * self.wide + 1 + self.n1)
        self.width_h = up128(max(MARGIN + 2 * self.wide + 1 + self.n2, MARGIN + self.n1))
        self.start = ((1 << b) - 1) * WIDTH


GEO = [Geo(b) for b in range(4)]
MAIN = 1536
SIDE = 256


def place():
    return lax.axis_index("branch"), lax.axis_index("row"), lax.axis_index("col")


def per_branch(body):
    branch = place()[0]
    for g in GEO:

        @pl.when(branch == g.b)
        def _(g=g):
            body(g)


def cols_kernel(x, west, east):
    def body(g):
        for q in range(g.parts):
            for y in range(g.rows):
                lane = q * g.pixels + y * g.cols
                at = 2 * (q * g.rows + y)
                west[:, at : at + 2] = x[:, lane : lane + 2]
                last = lane + g.cols - 2
                east[:, at : at + 2] = x[:, last : last + 2]

    per_branch(body)


def runs(g, k):
    i = 0
    while i < g.high:
        y = (k * g.strip - 2 + i) % g.rows
        n = min(g.high - i, g.rows - y)
        yield i, y, n
        i += n


def strips_kernel(x, out):
    def body(g):
        for k in range(4):
            for q in range(g.parts):
                for i, y, n in runs(g, k):
                    at = q * g.main + i * g.cols
                    lane = q * g.pixels + y * g.cols
                    out[k, :, at : at + n * g.cols] = x[:, lane : lane + n * g.cols]

    per_branch(body)


def sides_kernel(left, right, _, out):
    def body(g):
        for k in range(4):
            for q in range(g.parts):
                for i, y, n in runs(g, k):
                    at = q * g.side + 2 * i
                    lane = 2 * (q * g.rows + y)
                    out[k, :, at : at + 2 * n] = left[:, lane : lane + 2 * n]
                    at += 128
                    out[k, :, at : at + 2 * n] = right[:, lane : lane + 2 * n]

    per_branch(body)


def channel_order(g):
    out = lax.broadcasted_iota(jnp.int32, (g.channels, g.channels), 0)
    k = lax.broadcasted_iota(jnp.int32, (g.channels, g.channels), 1)
    part = jnp.zeros_like(k)
    for m in range(1, g.parts):
        part = part + (k >= WIDTH * m).astype(jnp.int32)
    at = (k - WIDTH * part) * g.parts + part
    return (at == out).astype(F32).astype(BF)


def inside(g, row_place, col_place):
    p = lax.broadcasted_iota(jnp.int32, (8, g.n1), 1).astype(F32)
    row = jnp.floor((p + 0.5) * (1.0 / g.wide))
    rest = p - row * g.wide
    tile = jnp.floor((rest + 0.5) * (1.0 / g.pitch))
    x = rest - tile * g.pitch
    y = row - 1.0 + (row_place * g.strip).astype(F32)
    outside = (
        ((tile == 0.0) & (y < 0.0))
        | ((tile == 3.0) & (y > g.rows - 1.0))
        | ((x == 1.0) & (col_place == 0))
        | ((x == g.cols + 2.0) & (col_place == 15))
    )
    return jnp.where(outside, 0.0, 1.0)[0:1, :]


def block_kernel(strips, sides, weight, bias, out, *scratch):
    wbuf, sems, wcat, col, z0 = scratch[:5]
    st_all = scratch[5:9]
    xp_all = scratch[9:13]
    hp_all = scratch[13:17]
    zt_all = (None,) + scratch[17:20]
    _, row_place, col_place = place()

    def body(g):
        c = g.channels
        cl = up128(c)

        def fetch(layer, dy):
            return pltpu.make_async_copy(
                weight.at[0, layer, dy, :, 0:c, 0:cl],
                wbuf.at[layer, dy, :, 0:c, 0:cl],
                sems.at[layer, dy],
            )

        for layer in range(2):
            for dy in range(3):
                fetch(layer, dy).start()

        st, xp, hp = st_all[g.b], xp_all[g.b], hp_all[g.b]
        ends = (0, g.main, g.main + g.side, g.main + 2 * g.side)

        def fill(tile, source, i=None):
            for q in range(g.parts):
                rows = slice(q * WIDTH, (q + 1) * WIDTH)
                for at, ref, lane, n in (
                    (ends[0], strips, q * g.main, g.cols),
                    (ends[1], sides, q * g.side, 2),
                    (ends[2], sides, 128 + q * g.side, 2),
                ):
                    first, size = (0, n * g.high) if i is None else (i * n, n)
                    at = tile * g.slot + at + first
                    if 0 <= source < 4:
                        piece = ref[source, :, lane + first : lane + first + size]
                    else:
                        piece = jnp.zeros((WIDTH, size), BF)
                    st[rows, at : at + size] = piece

        for tile in range(4):
            fill(tile, tile)
        for i in range(g.high):
            low = [k for k in range(4) if k * g.strip - 2 + i < 0]
            high = [k for k in range(4) if k * g.strip - 2 + i >= g.rows]
            if low:

                @pl.when(row_place <= max(low))
                def _(i=i):
                    for tile in range(4):
                        fill(tile, tile - 1, i)

            if high:

                @pl.when(row_place >= min(high))
                def _(i=i):
                    for tile in range(4):
                        fill(tile, tile + 1, i)

        if g.b:
            st[...] = jnp.dot(channel_order(g), st[...], preferred_element_type=F32).astype(BF)
        for i in range(g.high):
            for tile in range(4):
                at = MARGIN + i * g.wide + tile * g.pitch
                base = tile * g.slot
                for to, lane, n in (
                    (at, base + ends[1] + 2 * i, 2),
                    (at + 2, base + i * g.cols, g.cols),
                    (at + 2 + g.cols, base + ends[2] + 2 * i, 2),
                ):
                    xp[:, to : to + n] = st[:, lane : lane + n]

        mask = inside(g, row_place, col_place)

        def column(layer):
            wide = jnp.broadcast_to(bias[0, layer : layer + 1, :], (8, 8 * WIDTH))
            return wide.T[0:c, 0:1]

        def conv(layer, source, n, finish):
            total = None
            for dy in range(3):
                fetch(layer, dy).wait()
                for dx in range(3):
                    lane = MARGIN + dy * g.wide + dx - 1
                    if g.b == 0:
                        t = 3 * dy + dx
                        wcat[:, WIDTH * t : WIDTH * (t + 1)] = wbuf[layer, dy, dx, 0:c, 0:c]
                        col[WIDTH * t : WIDTH * (t + 1), 0:n] = source[:, lane : lane + n]
                    else:
                        term = jnp.dot(
                            wbuf[layer, dy, dx, 0:c, 0:c],
                            source[:, lane : lane + n],
                            preferred_element_type=F32,
                        )
                        total = term if total is None else total + term
            if g.b:
                finish(0, n, total)
                return
            for at in range(0, n, 384):
                size = min(384, n - at)
                finish(
                    at,
                    size,
                    jnp.dot(wcat[...], col[:, at : at + size], preferred_element_type=F32),
                )

        bias0 = column(0)

        def finish_first(at, size, total):
            h = jnp.maximum(total + bias0, 0.0) * mask[:, at : at + size]
            hp[:, MARGIN + at : MARGIN + at + size] = h.astype(BF)

        conv(0, xp, g.n1, finish_first)

        bias1 = column(1)

        def finish_second(at, size, total):
            lane = MARGIN + 2 * g.wide + at
            own = xp[:, lane : lane + size].astype(F32)
            z = jnp.maximum(total + bias1 + own, 0.0)
            if g.b == 0:
                z0[:, at : at + size] = z.astype(BF)
            else:
                zt_all[g.b][...] = z.T

        conv(1, hp, g.n2, finish_second)

        for tile in range(4):
            for i in range(g.strip):
                at = i * g.wide + tile * g.pitch + 2
                if g.b == 0:
                    out[tile, i * WIDTH : (i + 1) * WIDTH, :] = z0[:, at : at + g.cols]
                    continue
                values = zt_all[g.b][at : at + g.cols, :].astype(BF)
                for m in range(cl // 128):
                    r = (m * g.strip + i) * g.cols
                    lanes = min(128, c - 128 * m)
                    out[tile, r : r + g.cols, 0:lanes] = values[:, 128 * m : 128 * m + lanes]

    per_branch(body)


def repeat_map(j, i):
    gj, gi = GEO[j], GEO[i]
    shape = (gj.pixels // 4, gi.pixels // 4)
    fine = lax.broadcasted_iota(jnp.int32, shape, 0)
    coarse = lax.broadcasted_iota(jnp.int32, shape, 1)
    return cover(fine, coarse, gj, i - j)


def cover(fine, coarse, g, d):
    bits = 7 - g.b
    y = fine >> bits
    x = fine & (g.cols - 1)
    return (((y >> d) << (bits - d)) + (x >> d) == coarse).astype(F32).astype(BF)


def repeat_map_t(j, i):
    gj, gi = GEO[j], GEO[i]
    shape = (gi.pixels // 4, gj.pixels // 4)
    coarse = lax.broadcasted_iota(jnp.int32, shape, 0)
    fine = lax.broadcasted_iota(jnp.int32, shape, 1)
    return cover(fine, coarse, gj, i - j)


def nn(a, b):
    return jnp.dot(a, b, preferred_element_type=F32)


def nt(a, b):
    return lax.dot_general(a, b, (((1,), (1,)), ((), ())), preferred_element_type=F32)


def join_kernel(zb, weight, bias, out0, out1, out2, out3, z0s, s0):
    for y in range(8):
        z0s[:, 128 * y : 128 * (y + 1)] = zb[0, WIDTH * y : WIDTH * (y + 1), :]
    z = [
        z0s[...],
        zb[1, 0:256, 0:96],
        jnp.concatenate([zb[2, 0:64, :], zb[2, 64:128, 0:64]], axis=1),
        jnp.concatenate([zb[3, 0:16, :], zb[3, 16:32, :], zb[3, 32:48, :]], axis=1),
    ]

    def block(j, i):
        gj, gi = GEO[j], GEO[i]
        return weight[gj.start : gj.start + gj.channels, gi.start : gi.start + gi.channels]

    total = None
    for i in (1, 2, 3):
        term = nn(nt(block(0, i), z[i]).astype(BF), repeat_map_t(0, i))
        total = term if total is None else total + term
    wide = jnp.broadcast_to(bias[:, 0:WIDTH], (8, WIDTH))
    total = jnp.maximum(total + z[0].astype(F32) + wide.T[:, 0:1], 0.0)
    for y in range(8):
        s0[:, y, :] = total[:, 128 * y : 128 * (y + 1)]
    out0[...] = s0[...].astype(BF)

    for j, out in ((1, out1), (2, out2), (3, out3)):
        g = GEO[j]
        total = z[j].astype(F32) + bias[:, g.start : g.start + g.channels]
        for i in range(4):
            if i == j:
                continue
            if i < j:
                sums = (nt if i == 0 else nn)(repeat_map_t(i, j), z[i])
                mean = (sums * (0.25 ** (j - i))).astype(BF)
                total = total + nt(mean, block(j, i)).astype(BF).astype(F32)
            else:
                total = total + nn(repeat_map(j, i), nt(z[i], block(j, i)).astype(BF))
        out[...] = jnp.maximum(total, 0.0).astype(BF)


def params(mib=40):
    return pltpu.CompilerParams(vmem_limit_bytes=mib * 1024 * 1024)


def like(*shapes):
    return tuple(jax.ShapeDtypeStruct(s, BF) for s in shapes)


def call_cols(x):
    return pl.pallas_call(
        cols_kernel,
        out_shape=like((WIDTH, 128), (WIDTH, 128)),
        in_specs=[VMEM],
        out_specs=(VMEM, VMEM),
        compiler_params=params(),
    )(x)


def call_strips(x):
    return pl.pallas_call(
        strips_kernel,
        out_shape=like((4, WIDTH, MAIN))[0],
        in_specs=[VMEM],
        out_specs=VMEM,
        compiler_params=params(),
    )(x)


def call_sides(left, right, after):
    return pl.pallas_call(
        sides_kernel,
        out_shape=like((4, WIDTH, SIDE))[0],
        in_specs=[VMEM] * 2 + [pl.BlockSpec(memory_space=pl.ANY)],
        out_specs=VMEM,
        compiler_params=params(),
    )(left, right, after)


def call_block(strips, sides, weight, bias):
    scratch = [
        pltpu.VMEM((2, 3, 3, 384, 384), BF),
        pltpu.SemaphoreType.DMA((2, 3)),
        pltpu.VMEM((WIDTH, 9 * WIDTH), BF),
        pltpu.VMEM((9 * WIDTH, GEO[0].n1), BF),
        pltpu.VMEM((WIDTH, GEO[0].n2), BF),
    ]
    scratch += [pltpu.VMEM((g.channels, 4 * g.slot), BF) for g in GEO]
    scratch += [pltpu.VMEM((g.channels, g.width_x), BF) for g in GEO]
    scratch += [pltpu.VMEM((g.channels, g.width_h), BF) for g in GEO]
    scratch += [pltpu.VMEM((g.n2, g.channels), F32) for g in GEO[1:]]
    return pl.pallas_call(
        block_kernel,
        out_shape=like((4, 384, 128))[0],
        in_specs=[VMEM, VMEM, pl.BlockSpec(memory_space=pltpu.HBM), VMEM],
        out_specs=VMEM,
        scratch_shapes=scratch,
        compiler_params=params(60),
    )(strips, sides, weight, bias)


def call_join(received, weight, bias):
    return pl.pallas_call(
        join_kernel,
        out_shape=like((WIDTH, 8, 128), (256, 96), (64, 192), (16, 384)),
        in_specs=[VMEM] * 3,
        out_specs=(VMEM,) * 4,
        scratch_shapes=[
            pltpu.VMEM((WIDTH, 1024), BF),
            pltpu.VMEM((WIDTH, 8, 128), F32),
        ],
        compiler_params=params(),
    )(received, weight, bias)


def shifted(shard, axis, by):
    size = lax.axis_size(axis)
    pairs = [(i, i + by) for i in range(size) if 0 <= i + by < size]
    return lax.ppermute(shard, axis, pairs)


def swapped(parts, axis):
    return lax.all_to_all(parts, axis, split_axis=0, concat_axis=0, tiled=True)


def local(section_in, conv_weight, conv_bias, join_weight, join_bias):
    x = section_in[0, 0, 0]
    west, east = call_cols(x)
    left = shifted(east, "col", 1)
    right = shifted(west, "col", -1)
    strips = swapped(call_strips(x), "row")
    sides = swapped(call_sides(left, right, strips), "row")
    settled = call_block(strips, sides, conv_weight, conv_bias)
    out = call_join(swapped(settled, "branch"), join_weight, join_bias[None, :])
    first = [out[0]]
    for g in GEO[1:]:
        pixel_major = out[g.b].reshape(g.strip, g.cols, g.channels)
        first.append(pixel_major.transpose(2, 0, 1))
    return tuple(first)


def solution(mesh):
    in_specs = (
        P("branch", "row", "col", None, None),
        P("branch", None, None, None, None, None),
        P("branch", None, None),
        P(),
        P(),
    )
    out_specs = (P(None, ("branch", "row"), "col"),) * 4
    return jax.shard_map(local, mesh=mesh, in_specs=in_specs, out_specs=out_specs, check_vma=False)
```

```python
import jax
import jax.numpy as jnp
from jax import lax
from jax.experimental import pallas as pl
from jax.experimental.pallas import tpu as pltpu
from jax.sharding import PartitionSpec as P

WIDTH = 48
TH = 32
TW = 128
MARGIN = 128
BF = jnp.bfloat16
F32 = jnp.float32
VMEM = pl.BlockSpec(memory_space=pltpu.VMEM)


def up128(n):
    return -(-n // 128) * 128


class Geo:
    def __init__(self, b):
        self.b = b
        self.parts = 1 << b
        self.channels = WIDTH << b
        self.rows = TH >> b
        self.cols = TW >> b
        self.pixels = self.rows * self.cols
        self.strip = self.rows // 4
        self.high = self.strip + 4
        self.main = self.high * self.cols
        self.side = self.high * 2
        self.slot = up128(self.main + 2 * self.side)
        self.pitch = self.cols + 4
        self.wide = 4 * self.pitch
        self.n1 = up128((self.strip + 2) * self.wide)
        self.n2 = up128(self.strip * self.wide)
        self.width_x = up128(MARGIN + 2 * self.wide + 1 + self.n1)
        self.width_h = up128(max(MARGIN + 2 * self.wide + 1 + self.n2, MARGIN + self.n1))
        self.start = ((1 << b) - 1) * WIDTH


GEO = [Geo(b) for b in range(4)]
MAIN = 1536
STEPS = (384, 640, 384, 256)


def place():
    return lax.axis_index("branch"), lax.axis_index("row"), lax.axis_index("col")


def per_branch(body):
    branch = place()[0]
    for g in GEO:

        @pl.when(branch == g.b)
        def _(g=g):
            body(g)


def cols_kernel(strips, far, near):
    def body(g):
        size = g.parts * g.main
        n = g.parts * g.side
        rows = strips[:, :, 0:size].reshape(4 * WIDTH, size)
        k = lax.broadcasted_iota(jnp.int32, (size, n), 0)
        m = lax.broadcasted_iota(jnp.int32, (size, n), 1)
        first = k - (m >> 1) * g.cols - (m & 1)
        odd = place()[2] % 2
        for out, at_end in ((far, odd), (near, 1 - odd)):
            lane = at_end * (g.cols - 2)
            pick = (first == lane).astype(F32).astype(BF)
            out[:, 0:n] = jnp.dot(rows, pick, preferred_element_type=F32).astype(BF)

    per_branch(body)


def runs(g, k):
    i = 0
    while i < g.high:
        y = (k * g.strip - 2 + i) % g.rows
        n = min(g.high - i, g.rows - y)
        yield i, y, n
        i += n


def strips_kernel(x, out):
    def body(g):
        for k in range(4):
            for q in range(g.parts):
                for i, y, n in runs(g, k):
                    at = q * g.main + i * g.cols
                    lane = q * g.pixels + y * g.cols
                    out[k, :, at : at + n * g.cols] = x[:, lane : lane + n * g.cols]

    per_branch(body)


def channel_order(g):
    out = lax.broadcasted_iota(jnp.int32, (g.channels, g.channels), 0)
    k = lax.broadcasted_iota(jnp.int32, (g.channels, g.channels), 1)
    part = jnp.zeros_like(k)
    for m in range(1, g.parts):
        part = part + (k >= WIDTH * m).astype(jnp.int32)
    at = (k - WIDTH * part) * g.parts + part
    return (at == out).astype(F32).astype(BF)


def inside(g, row_place, col_place):
    p = lax.broadcasted_iota(jnp.int32, (8, g.n1), 1).astype(F32)
    row = jnp.floor((p + 0.5) * (1.0 / g.wide))
    rest = p - row * g.wide
    tile = jnp.floor((rest + 0.5) * (1.0 / g.pitch))
    x = rest - tile * g.pitch
    y = row - 1.0 + (row_place * g.strip).astype(F32)
    outside = (
        ((tile == 0.0) & (y < 0.0))
        | ((tile == 3.0) & (y > g.rows - 1.0))
        | ((x == 1.0) & (col_place == 0))
        | ((x == g.cols + 2.0) & (col_place == 15))
    )
    return jnp.where(outside, 0.0, 1.0)[0:1, :]


def side_places(g, row_place):
    shape = (8 * g.side, g.width_x)
    n = lax.broadcasted_iota(jnp.int32, (1, g.width_x), 1).astype(F32) - MARGIN
    row = jnp.floor((n + 0.5) * (1.0 / g.wide))
    rest = n - row * g.wide
    tile = jnp.floor((rest + 0.5) * (1.0 / g.pitch))
    x = rest - tile * g.pitch
    y = row - 2.0 + (row_place * g.strip).astype(F32)
    tile = tile + jnp.where(y < 0.0, -1.0, 0.0) + jnp.where(y > g.rows - 1.0, 1.0, 0.0)
    right = x > g.cols + 1.0
    spot = jnp.where(right, x - (g.cols + 2.0), x) + 2.0 * row + g.side * tile
    spot = spot + jnp.where(right, 4.0 * g.side, 0.0)
    known = (x < 2.0) | right
    known = known & (row > -1.0) & (row < g.high) & (tile > -1.0) & (tile < 4.0)
    spot = jnp.where(known, spot, -1.0)
    k = lax.broadcasted_iota(jnp.int32, shape, 0).astype(F32)
    return (k == spot).astype(F32).astype(BF)


def prepare_kernel(strips, weight, _, *refs):
    xp_all, wp_all, orders, places, st_all = refs[:4], refs[4:8], refs[8:11], refs[11:14], refs[14:]
    row_place = place()[1]

    def body(g):
        c = g.channels
        st, xp, wp = st_all[g.b], xp_all[g.b], wp_all[g.b]

        def fill(tile, source, i=None):
            for q in range(g.parts):
                first, size = (0, g.main) if i is None else (i * g.cols, g.cols)
                at = tile * g.slot + first
                lane = q * g.main + first
                if 0 <= source < 4:
                    piece = strips[source, :, lane : lane + size]
                else:
                    piece = jnp.zeros((WIDTH, size), BF)
                st[q * WIDTH : (q + 1) * WIDTH, at : at + size] = piece

        for tile in range(4):
            fill(tile, tile)
        for i in range(g.high):
            low, high = outside(g, i)
            if low:

                @pl.when(row_place <= max(low))
                def _(i=i):
                    for tile in range(4):
                        fill(tile, tile - 1, i)

            if high:

                @pl.when(row_place >= min(high))
                def _(i=i):
                    for tile in range(4):
                        fill(tile, tile + 1, i)

        if g.b:
            order = channel_order(g)
            orders[g.b - 1][...] = order
            places[g.b - 1][...] = side_places(g, row_place)
            st[...] = jnp.dot(order, st[...], preferred_element_type=F32).astype(BF)
        xp[...] = jnp.zeros_like(xp)
        for i in range(g.high):
            for tile in range(4):
                to = MARGIN + i * g.wide + tile * g.pitch + 2
                lane = tile * g.slot + i * g.cols
                xp[:, to : to + g.cols] = st[:, lane : lane + g.cols]
        for layer in range(2):
            for dy in range(3):
                for dx in range(3):
                    t = 3 * dy + dx
                    wp[layer, :, c * t : c * (t + 1)] = weight[0, layer, dy, dx, 0:c, 0:c]

    per_branch(body)


def outside(g, i):
    low = [k for k in range(4) if k * g.strip - 2 + i < 0]
    high = [k for k in range(4) if k * g.strip - 2 + i >= g.rows]
    return low, high


def block_kernel(far, near, bias, *refs):
    xp_all, wp_all, orders, places = refs[:4], refs[4:8], refs[8:11], refs[11:14]
    out, refs = refs[14], refs[15:]
    xs_all, col_all, hp_all, st_all, (z0,) = refs[:4], refs[4:8], refs[8:12], refs[12:15], refs[15:16]
    zt_all, left, right = refs[16:19], refs[19], refs[20]
    _, row_place, col_place = place()

    @pl.when(col_place % 2 == 0)
    def _():
        left[...] = far[...]
        right[...] = near[...]

    @pl.when(col_place % 2 == 1)
    def _():
        left[...] = near[...]
        right[...] = far[...]

    def body(g):
        c = g.channels
        cl = up128(c)
        xp, hp, wp, col = xs_all[g.b], hp_all[g.b], wp_all[g.b], col_all[g.b]
        if g.b == 0:
            xp[...] = xp_all[0][...]

            def sides(i, tile, source):
                at = MARGIN + i * g.wide + tile * g.pitch
                for ref, to in ((left, at), (right, at + 2 + g.cols)):
                    if 0 <= source < 4:
                        piece = ref[source * WIDTH : (source + 1) * WIDTH, 2 * i : 2 * i + 2]
                    else:
                        piece = jnp.zeros((WIDTH, 2), BF)
                    xp[:, to : to + 2] = piece

            for i in range(g.high):
                low, high = outside(g, i)
                for tile in range(4):
                    sides(i, tile, tile)
                if low:

                    @pl.when(row_place <= max(low))
                    def _(i=i):
                        for tile in range(4):
                            sides(i, tile, tile - 1)

                if high:

                    @pl.when(row_place >= min(high))
                    def _(i=i):
                        for tile in range(4):
                            sides(i, tile, tile + 1)

        else:
            st = st_all[g.b - 1]
            for q in range(g.parts):
                for s, ref in enumerate((left, right)):
                    for tile in range(4):
                        at = (4 * s + tile) * g.side
                        st[q * WIDTH : (q + 1) * WIDTH, at : at + g.side] = ref[
                            tile * WIDTH : (tile + 1) * WIDTH, q * g.side : (q + 1) * g.side
                        ]
            stacked = nn(orders[g.b - 1][...], st[...]).astype(BF)
            xp[...] = xp_all[g.b][...] + nn(stacked, places[g.b - 1][...]).astype(BF)

        mask = inside(g, row_place, col_place)

        def column(layer):
            wide = jnp.broadcast_to(bias[0, layer : layer + 1, :], (8, 8 * WIDTH))
            return wide.T[0:c, 0:1]

        def conv(layer, source, n, finish):
            for dy in range(3):
                for dx in range(3):
                    lane = MARGIN + dy * g.wide + dx - 1
                    t = 3 * dy + dx
                    col[c * t : c * (t + 1), 0:n] = source[:, lane : lane + n]
            step = STEPS[g.b]
            for at in range(0, n, step):
                size = min(step, n - at)
                finish(at, size, nn(wp[layer], col[:, at : at + size]))

        bias0 = column(0)

        def finish_first(at, size, total):
            h = jnp.maximum(total + bias0, 0.0) * mask[:, at : at + size]
            hp[:, MARGIN + at : MARGIN + at + size] = h.astype(BF)

        conv(0, xp, g.n1, finish_first)

        bias1 = column(1)

        def finish_second(at, size, total):
            lane = MARGIN + 2 * g.wide + at
            own = xp[:, lane : lane + size].astype(F32)
            z = jnp.maximum(total + bias1 + own, 0.0)
            if g.b == 0:
                z0[:, at : at + size] = z.astype(BF)
            else:
                zt_all[g.b - 1][at : at + size, :] = z.T

        conv(1, hp, g.n2, finish_second)

        for tile in range(4):
            for i in range(g.strip):
                at = i * g.wide + tile * g.pitch + 2
                if g.b == 0:
                    out[tile, i * WIDTH : (i + 1) * WIDTH, :] = z0[:, at : at + g.cols]
                    continue
                values = zt_all[g.b - 1][at : at + g.cols, :].astype(BF)
                for m in range(cl // 128):
                    r = (m * g.strip + i) * g.cols
                    lanes = min(128, c - 128 * m)
                    out[tile, r : r + g.cols, 0:lanes] = values[:, 128 * m : 128 * m + lanes]

    per_branch(body)


def repeat_map(j, i):
    gj, gi = GEO[j], GEO[i]
    shape = (gj.pixels // 4, gi.pixels // 4)
    fine = lax.broadcasted_iota(jnp.int32, shape, 0)
    coarse = lax.broadcasted_iota(jnp.int32, shape, 1)
    return cover(fine, coarse, gj, i - j)


def cover(fine, coarse, g, d):
    bits = 7 - g.b
    y = fine >> bits
    x = fine & (g.cols - 1)
    return (((y >> d) << (bits - d)) + (x >> d) == coarse).astype(F32).astype(BF)


def repeat_map_t(j, i):
    gj, gi = GEO[j], GEO[i]
    shape = (gi.pixels // 4, gj.pixels // 4)
    coarse = lax.broadcasted_iota(jnp.int32, shape, 0)
    fine = lax.broadcasted_iota(jnp.int32, shape, 1)
    return cover(fine, coarse, gj, i - j)


def nn(a, b):
    return jnp.dot(a, b, preferred_element_type=F32)


def nt(a, b):
    return lax.dot_general(a, b, (((1,), (1,)), ((), ())), preferred_element_type=F32)


def join_kernel(zb, weight, bias, out0, out1, out2, out3, z0s, s0):
    for y in range(8):
        z0s[:, 128 * y : 128 * (y + 1)] = zb[0, WIDTH * y : WIDTH * (y + 1), :]
    z = [
        z0s[...],
        zb[1, 0:256, 0:96],
        jnp.concatenate([zb[2, 0:64, :], zb[2, 64:128, 0:64]], axis=1),
        jnp.concatenate([zb[3, 0:16, :], zb[3, 16:32, :], zb[3, 32:48, :]], axis=1),
    ]

    def block(j, i):
        gj, gi = GEO[j], GEO[i]
        return weight[gj.start : gj.start + gj.channels, gi.start : gi.start + gi.channels]

    total = None
    for i in (1, 2, 3):
        term = nn(nt(block(0, i), z[i]).astype(BF), repeat_map_t(0, i))
        total = term if total is None else total + term
    wide = jnp.broadcast_to(bias[:, 0:WIDTH], (8, WIDTH))
    total = jnp.maximum(total + z[0].astype(F32) + wide.T[:, 0:1], 0.0)
    for y in range(8):
        s0[:, y, :] = total[:, 128 * y : 128 * (y + 1)]
    out0[...] = s0[...].astype(BF)

    for j, out in ((1, out1), (2, out2), (3, out3)):
        g = GEO[j]
        total = z[j].astype(F32) + bias[:, g.start : g.start + g.channels]
        for i in range(4):
            if i == j:
                continue
            if i < j:
                sums = (nt if i == 0 else nn)(repeat_map_t(i, j), z[i])
                mean = (sums * (0.25 ** (j - i))).astype(BF)
                total = total + nt(mean, block(j, i)).astype(BF).astype(F32)
            else:
                total = total + nn(repeat_map(j, i), nt(z[i], block(j, i)).astype(BF))
        out[...] = jnp.maximum(total, 0.0).astype(BF)


def params(mib=40):
    return pltpu.CompilerParams(vmem_limit_bytes=mib * 1024 * 1024)


def like(*shapes):
    return tuple(jax.ShapeDtypeStruct(s, BF) for s in shapes)


def call_cols(strips):
    return pl.pallas_call(
        cols_kernel,
        out_shape=like((4 * WIDTH, 128), (4 * WIDTH, 128)),
        in_specs=[VMEM],
        out_specs=(VMEM, VMEM),
        compiler_params=params(),
    )(strips)


def call_strips(x):
    return pl.pallas_call(
        strips_kernel,
        out_shape=like((4, WIDTH, MAIN))[0],
        in_specs=[VMEM],
        out_specs=VMEM,
        compiler_params=params(),
    )(x)


def prepared_shapes():
    shapes = [(g.channels, g.width_x) for g in GEO]
    shapes += [(2, g.channels, 9 * g.channels) for g in GEO]
    shapes += [(g.channels, g.channels) for g in GEO[1:]]
    shapes += [(8 * g.side, g.width_x) for g in GEO[1:]]
    return shapes


def call_prepare(strips, weight, after):
    shapes = prepared_shapes()
    return pl.pallas_call(
        prepare_kernel,
        out_shape=like(*shapes),
        in_specs=[VMEM, VMEM, pl.BlockSpec(memory_space=pl.ANY)],
        out_specs=(VMEM,) * len(shapes),
        scratch_shapes=[pltpu.VMEM((g.channels, 4 * g.slot), BF) for g in GEO],
        compiler_params=params(),
        cost_estimate=pl.CostEstimate(flops=10**9, bytes_accessed=12 * 2**20, transcendentals=0),
    )(strips, weight, after)


def call_block(far, near, bias, prepared):
    scratch = [pltpu.VMEM((g.channels, g.width_x), BF) for g in GEO]
    scratch += [pltpu.VMEM((9 * g.channels, g.n1), BF) for g in GEO]
    scratch += [pltpu.VMEM((g.channels, g.width_h), BF) for g in GEO]
    scratch += [pltpu.VMEM((g.channels, 8 * g.side), BF) for g in GEO[1:]]
    scratch += [pltpu.VMEM((WIDTH, GEO[0].n2), BF)]
    scratch += [pltpu.VMEM((g.n2, g.channels), F32) for g in GEO[1:]]
    scratch += [pltpu.VMEM((4 * WIDTH, 128), BF)] * 2
    return pl.pallas_call(
        block_kernel,
        out_shape=like((4, 384, 128))[0],
        in_specs=[VMEM] * (3 + len(prepared)),
        out_specs=VMEM,
        scratch_shapes=scratch,
        compiler_params=params(),
    )(far, near, bias, *prepared)


def call_join(received, weight, bias):
    return pl.pallas_call(
        join_kernel,
        out_shape=like((WIDTH, 8, 128), (256, 96), (64, 192), (16, 384)),
        in_specs=[VMEM] * 3,
        out_specs=(VMEM,) * 4,
        scratch_shapes=[
            pltpu.VMEM((WIDTH, 1024), BF),
            pltpu.VMEM((WIDTH, 8, 128), F32),
        ],
        compiler_params=params(),
    )(received, weight, bias)


def paired(shard, first):
    size = lax.axis_size("col")
    pairs = []
    for c in range(first, size - 1, 2):
        pairs += [(c, c + 1), (c + 1, c)]
    return lax.ppermute(shard, "col", pairs)


def swapped(parts, axis):
    return lax.all_to_all(parts, axis, split_axis=0, concat_axis=0, tiled=True)


def local(section_in, conv_weight, conv_bias, join_weight, join_bias):
    x = section_in[0, 0, 0]
    strips = swapped(call_strips(x), "row")
    far, near = call_cols(strips)
    prepared = call_prepare(strips, conv_weight, far)
    settled = call_block(paired(far, 1), paired(near, 0), conv_bias, prepared)
    out = call_join(swapped(settled, "branch"), join_weight, join_bias[None, :])
    first = [out[0]]
    for g in GEO[1:]:
        pixel_major = out[g.b].reshape(g.strip, g.cols, g.channels)
        first.append(pixel_major.transpose(2, 0, 1))
    return tuple(first)


def solution(mesh):
    in_specs = (
        P("branch", "row", "col", None, None),
        P("branch", None, None, None, None, None),
        P("branch", None, None),
        P(),
        P(),
    )
    out_specs = (P(None, ("branch", "row"), "col"),) * 4
    return jax.shard_map(local, mesh=mesh, in_specs=in_specs, out_specs=out_specs, check_vma=False)
```

```python
import jax
import jax.numpy as jnp
from jax import lax
from jax.experimental import pallas as pl
from jax.experimental.pallas import tpu as pltpu
from jax.sharding import PartitionSpec as P

WIDTH = 48
TH = 32
TW = 128
MARGIN = 128
BF = jnp.bfloat16
F32 = jnp.float32
VMEM = pl.BlockSpec(memory_space=pltpu.VMEM)


def up128(n):
    return -(-n // 128) * 128


class Geo:
    def __init__(self, b):
        self.b = b
        self.parts = 1 << b
        self.channels = WIDTH << b
        self.rows = TH >> b
        self.cols = TW >> b
        self.pixels = self.rows * self.cols
        self.strip = self.rows // 4
        self.high = self.strip + 4
        self.pitch = self.cols + 4
        self.padded = up128(self.rows * self.pitch)
        self.sides = 4 * self.rows
        self.slot = up128(self.high * self.pitch + 2)
        self.blocks = self.slot // 128
        self.tile_h = (self.strip + 2) * self.pitch
        self.tile_z = self.strip * self.pitch
        self.n1 = up128(4 * self.tile_h)
        self.n2 = up128(4 * self.tile_z)
        self.width_h = up128(2 * MARGIN + self.n1)
        self.start = ((1 << b) - 1) * WIDTH


GEO = [Geo(b) for b in range(4)]
SLOT_ROWS = 624
STEPS = (384, 640, 384, 256)


def place():
    return lax.axis_index("branch"), lax.axis_index("row"), lax.axis_index("col")


def per_branch(body):
    branch = place()[0]
    for g in GEO:

        @pl.when(branch == g.b)
        def _(g=g):
            body(g)


def cols_kernel(x, far, near, west, east):
    def body(g):
        for q in range(g.parts):
            for y in range(g.rows):
                lane = q * g.pixels + y * g.cols
                at = 2 * (q * g.rows + y)
                west[:, at : at + 2] = x[:, lane : lane + 2]
                last = lane + g.cols - 2
                east[:, at : at + 2] = x[:, last : last + 2]

    per_branch(body)
    odd = place()[2] % 2

    @pl.when(odd == 0)
    def _():
        far[...] = west[...]
        near[...] = east[...]

    @pl.when(odd == 1)
    def _():
        far[...] = east[...]
        near[...] = west[...]


def channel_order(g):
    out = lax.broadcasted_iota(jnp.int32, (g.channels, g.channels), 0)
    k = lax.broadcasted_iota(jnp.int32, (g.channels, g.channels), 1)
    part = jnp.zeros_like(k)
    for m in range(1, g.parts):
        part = part + (k >= WIDTH * m).astype(jnp.int32)
    at = (k - WIDTH * part) * g.parts + part
    return (at == out).astype(F32).astype(BF)


def side_places(g):
    n = lax.broadcasted_iota(jnp.int32, (1, g.padded), 1).astype(F32)
    y = jnp.floor((n + 0.5) * (1.0 / g.pitch))
    x = n - y * g.pitch
    right = x > g.cols + 1.0
    spot = 2.0 * y + jnp.where(right, x - (g.cols + 2.0) + 2.0 * g.rows, x)
    spot = jnp.where(((x < 2.0) | right) & (y < g.rows), spot, -1.0)
    k = lax.broadcasted_iota(jnp.int32, (g.sides, g.padded), 0).astype(F32)
    return (k == spot).astype(F32).astype(BF)


def prepare_kernel(x, weight, _, *refs):
    xp_all, wp_all, places, orders = refs[:4], refs[4:8], refs[8:12], (None,) + refs[12:15]
    st_all = (x,) + refs[15:18]

    def body(g):
        c = g.channels
        st, xp, wp = st_all[g.b], xp_all[g.b], wp_all[g.b]
        places[g.b][...] = side_places(g)
        if g.b:
            order = channel_order(g)
            orders[g.b][...] = order
            for q in range(g.parts):
                st[q * WIDTH : (q + 1) * WIDTH, :] = x[:, q * g.pixels : (q + 1) * g.pixels]
            st[...] = nn(order, st[...]).astype(BF)
        xp[...] = jnp.zeros_like(xp)
        for y in range(g.rows):
            to = y * g.pitch + 2
            xp[:, to : to + g.cols] = st[:, y * g.cols : (y + 1) * g.cols]
        for layer in range(2):
            for dy in range(3):
                for dx in range(3):
                    t = 3 * dy + dx
                    wp[layer, :, c * t : c * (t + 1)] = weight[0, layer, dy, dx, 0:c, 0:c]

    per_branch(body)


def runs(g, k):
    i = 0
    while i < g.high:
        y = (k * g.strip - 2 + i) % g.rows
        n = min(g.high - i, g.rows - y)
        yield i, y, n
        i += n


def strips_kernel(far, near, *refs):
    xp_all, places, orders, out = refs[:4], refs[4:8], (None,) + refs[8:11], refs[11]
    left, right = refs[12:14]
    st_all, xf_all, slot_all = refs[14:18], refs[18:22], refs[22:26]
    odd = place()[2] % 2

    @pl.when(odd == 0)
    def _():
        left[...] = far[...]
        right[...] = near[...]

    @pl.when(odd == 1)
    def _():
        left[...] = near[...]
        right[...] = far[...]

    def body(g):
        c, n = g.channels, 2 * g.rows
        st, xf, slot = st_all[g.b], xf_all[g.b], slot_all[g.b]
        for q in range(g.parts):
            for s, ref in enumerate((left, right)):
                st[q * WIDTH : (q + 1) * WIDTH, s * n : (s + 1) * n] = ref[:, q * n : (q + 1) * n]
        stacked = st[...]
        if g.b:
            stacked = nn(orders[g.b][...], stacked).astype(BF)
        xf[...] = xp_all[g.b][...] + nn(stacked, places[g.b][...]).astype(BF)
        for k in range(4):
            for i, y, rows in runs(g, k):
                at, lane, size = 1 + i * g.pitch, y * g.pitch, rows * g.pitch
                slot[:, at : at + size] = xf[:, lane : lane + size]
            for m in range(g.blocks):
                out[k, m * c : (m + 1) * c, :] = slot[:, 128 * m : 128 * (m + 1)]

    per_branch(body)


def inside(g, row_place, col_place):
    p = lax.broadcasted_iota(jnp.int32, (8, g.n1), 1).astype(F32)
    tile = jnp.floor((p + 0.5) * (1.0 / g.tile_h))
    rest = p - tile * g.tile_h
    row = jnp.floor((rest + 0.5) * (1.0 / g.pitch))
    x = rest - row * g.pitch
    y = row - 1.0 + (row_place * g.strip).astype(F32)
    out = (
        ((tile == 0.0) & (y < 0.0))
        | ((tile == 3.0) & (y > g.rows - 1.0))
        | ((x == 1.0) & (col_place == 0))
        | ((x == g.cols + 2.0) & (col_place == 15))
    )
    return jnp.where(out, 0.0, 1.0)[0:1, :]


def block_kernel(strips, bias, *refs):
    wp_all, out = refs[:4], refs[4]
    xs_all, col_all, hp_all, own_all = refs[5:9], refs[9:13], refs[13:17], refs[17:21]
    z0, zt_all = refs[21], (None,) + refs[22:25]
    _, row_place, col_place = place()

    def body(g):
        c = g.channels
        cl = up128(c)
        xs, hp, wp, col, own = xs_all[g.b], hp_all[g.b], wp_all[g.b], col_all[g.b], own_all[g.b]
        for tile in range(4):
            for m in range(g.blocks):
                xs[tile, :, 128 * m : 128 * (m + 1)] = strips[tile, m * c : (m + 1) * c, :]
        for i in range(g.high):
            lanes = slice(1 + i * g.pitch, 1 + (i + 1) * g.pitch)
            low = [k for k in range(4) if k * g.strip - 2 + i < 0]
            high = [k for k in range(4) if k * g.strip - 2 + i >= g.rows]
            if low:

                @pl.when(row_place <= max(low))
                def _(lanes=lanes):
                    for tile in (3, 2, 1):
                        xs[tile, :, lanes] = xs[tile - 1, :, lanes]
                    xs[0, :, lanes] = jnp.zeros((c, g.pitch), BF)

            if high:

                @pl.when(row_place >= min(high))
                def _(lanes=lanes):
                    for tile in (0, 1, 2):
                        xs[tile, :, lanes] = xs[tile + 1, :, lanes]
                    xs[3, :, lanes] = jnp.zeros((c, g.pitch), BF)

        for tile in range(4):
            lane = 1 + 2 * g.pitch
            own[:, tile * g.tile_z : (tile + 1) * g.tile_z] = xs[tile, :, lane : lane + g.tile_z]

        mask = inside(g, row_place, col_place)

        def column(layer):
            wide = jnp.broadcast_to(bias[0, layer : layer + 1, :], (8, 8 * WIDTH))
            return wide.T[0:c, 0:1]

        def conv(layer, view, size, n, finish):
            for dy in range(3):
                for dx in range(3):
                    t = 3 * dy + dx
                    for tile in range(4):
                        col[c * t : c * (t + 1), tile * size : (tile + 1) * size] = view(
                            tile, dy * g.pitch + dx
                        )
            step = STEPS[g.b]
            for at in range(0, n, step):
                width = min(step, n - at)
                finish(at, width, nn(wp[layer], col[:, at : at + width]))

        bias0 = column(0)

        def finish_first(at, size, total):
            h = jnp.maximum(total + bias0, 0.0) * mask[:, at : at + size]
            hp[:, MARGIN + at : MARGIN + at + size] = h.astype(BF)

        conv(0, lambda tile, lane: xs[tile, :, lane : lane + g.tile_h], g.tile_h, g.n1, finish_first)

        bias1 = column(1)

        def finish_second(at, size, total):
            z = jnp.maximum(total + bias1 + own[:, at : at + size].astype(F32), 0.0)
            if g.b == 0:
                z0[:, at : at + size] = z.astype(BF)
            else:
                zt_all[g.b][at : at + size, :] = z.T

        def hidden(tile, lane):
            lane += MARGIN + tile * g.tile_h - 1
            return hp[:, lane : lane + g.tile_z]

        conv(1, hidden, g.tile_z, g.n2, finish_second)

        for tile in range(4):
            for i in range(g.strip):
                at = tile * g.tile_z + i * g.pitch + 2
                if g.b == 0:
                    out[tile, i * WIDTH : (i + 1) * WIDTH, :] = z0[:, at : at + g.cols]
                    continue
                values = zt_all[g.b][at : at + g.cols, :].astype(BF)
                for m in range(cl // 128):
                    r = (m * g.strip + i) * g.cols
                    lanes = min(128, c - 128 * m)
                    out[tile, r : r + g.cols, 0:lanes] = values[:, 128 * m : 128 * m + lanes]

    per_branch(body)


def repeat_map(j, i):
    gj, gi = GEO[j], GEO[i]
    shape = (gj.pixels // 4, gi.pixels // 4)
    fine = lax.broadcasted_iota(jnp.int32, shape, 0)
    coarse = lax.broadcasted_iota(jnp.int32, shape, 1)
    return cover(fine, coarse, gj, i - j)


def cover(fine, coarse, g, d):
    bits = 7 - g.b
    y = fine >> bits
    x = fine & (g.cols - 1)
    return (((y >> d) << (bits - d)) + (x >> d) == coarse).astype(F32).astype(BF)


def repeat_map_t(j, i):
    gj, gi = GEO[j], GEO[i]
    shape = (gi.pixels // 4, gj.pixels // 4)
    coarse = lax.broadcasted_iota(jnp.int32, shape, 0)
    fine = lax.broadcasted_iota(jnp.int32, shape, 1)
    return cover(fine, coarse, gj, i - j)


def nn(a, b):
    return jnp.dot(a, b, preferred_element_type=F32)


def nt(a, b):
    return lax.dot_general(a, b, (((1,), (1,)), ((), ())), preferred_element_type=F32)


def join_kernel(zb, weight, bias, out0, out1, out2, out3, z0s, s0):
    for y in range(8):
        z0s[:, 128 * y : 128 * (y + 1)] = zb[0, WIDTH * y : WIDTH * (y + 1), :]
    z = [
        z0s[...],
        zb[1, 0:256, 0:96],
        jnp.concatenate([zb[2, 0:64, :], zb[2, 64:128, 0:64]], axis=1),
        jnp.concatenate([zb[3, 0:16, :], zb[3, 16:32, :], zb[3, 32:48, :]], axis=1),
    ]

    def block(j, i):
        gj, gi = GEO[j], GEO[i]
        return weight[gj.start : gj.start + gj.channels, gi.start : gi.start + gi.channels]

    total = None
    for i in (1, 2, 3):
        term = nn(nt(block(0, i), z[i]).astype(BF), repeat_map_t(0, i))
        total = term if total is None else total + term
    wide = jnp.broadcast_to(bias[:, 0:WIDTH], (8, WIDTH))
    total = jnp.maximum(total + z[0].astype(F32) + wide.T[:, 0:1], 0.0)
    for y in range(8):
        s0[:, y, :] = total[:, 128 * y : 128 * (y + 1)]
    out0[...] = s0[...].astype(BF)

    for j, out in ((1, out1), (2, out2), (3, out3)):
        g = GEO[j]
        total = z[j].astype(F32) + bias[:, g.start : g.start + g.channels]
        for i in range(4):
            if i == j:
                continue
            if i < j:
                sums = (nt if i == 0 else nn)(repeat_map_t(i, j), z[i])
                mean = (sums * (0.25 ** (j - i))).astype(BF)
                total = total + nt(mean, block(j, i)).astype(BF).astype(F32)
            else:
                total = total + nn(repeat_map(j, i), nt(z[i], block(j, i)).astype(BF))
        out[...] = jnp.maximum(total, 0.0).astype(BF)


def params(mib=24):
    return pltpu.CompilerParams(vmem_limit_bytes=mib * 1024 * 1024)


def like(*shapes):
    return tuple(jax.ShapeDtypeStruct(s, BF) for s in shapes)


def call_cols(x):
    return pl.pallas_call(
        cols_kernel,
        out_shape=like((WIDTH, 128), (WIDTH, 128)),
        in_specs=[VMEM],
        out_specs=(VMEM, VMEM),
        scratch_shapes=[pltpu.VMEM((WIDTH, 128), BF)] * 2,
        compiler_params=params(),
    )(x)


def call_prepare(x, weight, after):
    shapes = [(g.channels, g.padded) for g in GEO]
    shapes += [(2, g.channels, 9 * g.channels) for g in GEO]
    shapes += [(g.sides, g.padded) for g in GEO]
    shapes += [(g.channels, g.channels) for g in GEO[1:]]
    made = pl.pallas_call(
        prepare_kernel,
        out_shape=like(*shapes),
        in_specs=[VMEM, VMEM, pl.BlockSpec(memory_space=pl.ANY)],
        out_specs=(VMEM,) * len(shapes),
        scratch_shapes=[pltpu.VMEM((g.channels, g.pixels), BF) for g in GEO[1:]],
        compiler_params=params(),
        cost_estimate=pl.CostEstimate(flops=10**9, bytes_accessed=12 * 2**20, transcendentals=0),
    )(x, weight, after)
    return made[:4] + made[8:], made[4:8]


def call_strips(far, near, padded):
    scratch = [pltpu.VMEM((WIDTH, 128), BF)] * 2
    scratch += [pltpu.VMEM((g.channels, g.sides), BF) for g in GEO]
    scratch += [pltpu.VMEM((g.channels, g.padded), BF) for g in GEO]
    scratch += [pltpu.VMEM((g.channels, g.slot), BF) for g in GEO]
    return pl.pallas_call(
        strips_kernel,
        out_shape=like((4, SLOT_ROWS, 128))[0],
        in_specs=[VMEM] * (2 + len(padded)),
        out_specs=VMEM,
        scratch_shapes=scratch,
        compiler_params=params(),
    )(far, near, *padded)


def call_block(strips, bias, weights):
    scratch = [pltpu.VMEM((4, g.channels, g.slot), BF) for g in GEO]
    scratch += [pltpu.VMEM((9 * g.channels, g.n1), BF) for g in GEO]
    scratch += [pltpu.VMEM((g.channels, g.width_h), BF) for g in GEO]
    scratch += [pltpu.VMEM((g.channels, g.n2), BF) for g in GEO]
    scratch += [pltpu.VMEM((WIDTH, GEO[0].n2), BF)]
    scratch += [pltpu.VMEM((g.n2, g.channels), F32) for g in GEO[1:]]
    return pl.pallas_call(
        block_kernel,
        out_shape=like((4, 384, 128))[0],
        in_specs=[VMEM] * 6,
        out_specs=VMEM,
        scratch_shapes=scratch,
        compiler_params=params(),
    )(strips, bias, *weights)


def call_join(received, weight, bias):
    return pl.pallas_call(
        join_kernel,
        out_shape=like((WIDTH, 8, 128), (256, 96), (64, 192), (16, 384)),
        in_specs=[VMEM] * 3,
        out_specs=(VMEM,) * 4,
        scratch_shapes=[
            pltpu.VMEM((WIDTH, 1024), BF),
            pltpu.VMEM((WIDTH, 8, 128), F32),
        ],
        compiler_params=params(),
    )(received, weight, bias)


def paired(shard, first):
    size = lax.axis_size("col")
    pairs = []
    for c in range(first, size - 1, 2):
        pairs += [(c, c + 1), (c + 1, c)]
    return lax.ppermute(shard, "col", pairs)


def swapped(parts, axis):
    return lax.all_to_all(parts, axis, split_axis=0, concat_axis=0, tiled=True)


def local(section_in, conv_weight, conv_bias, join_weight, join_bias):
    x = section_in[0, 0, 0]
    far, near = call_cols(x)
    padded, weights = call_prepare(x, conv_weight, far)
    strips = call_strips(paired(far, 1), paired(near, 0), padded)
    settled = call_block(swapped(strips, "row"), conv_bias, weights)
    out = call_join(swapped(settled, "branch"), join_weight, join_bias[None, :])
    first = [out[0]]
    for g in GEO[1:]:
        pixel_major = out[g.b].reshape(g.strip, g.cols, g.channels)
        first.append(pixel_major.transpose(2, 0, 1))
    return tuple(first)


def solution(mesh):
    in_specs = (
        P("branch", "row", "col", None, None),
        P("branch", None, None, None, None, None),
        P("branch", None, None),
        P(),
        P(),
    )
    out_specs = (P(None, ("branch", "row"), "col"),) * 4
    return jax.shard_map(local, mesh=mesh, in_specs=in_specs, out_specs=out_specs, check_vma=False)
```

```python
import jax
import jax.numpy as jnp
from jax import lax
from jax.experimental import pallas as pl
from jax.experimental.pallas import tpu as pltpu
from jax.sharding import PartitionSpec as P

WIDTH = 48
TH = 32
TW = 128
MARGIN = 128
BF = jnp.bfloat16
F32 = jnp.float32
VMEM = pl.BlockSpec(memory_space=pltpu.VMEM)


def up128(n):
    return -(-n // 128) * 128


class Geo:
    def __init__(self, b):
        self.b = b
        self.parts = 1 << b
        self.channels = WIDTH << b
        self.rows = TH >> b
        self.cols = TW >> b
        self.pixels = self.rows * self.cols
        self.strip = self.rows // 4
        self.high = self.strip + 4
        self.pitch = self.cols + 4
        self.padded = up128(self.rows * self.pitch)
        self.sides = 4 * self.rows
        self.slot = up128(self.high * self.pitch + 2)
        self.blocks = self.slot // 128
        self.tile_h = (self.strip + 2) * self.pitch
        self.tile_z = self.strip * self.pitch
        self.n1 = up128(4 * self.tile_h)
        self.n2 = up128(4 * self.tile_z)
        self.width_h = up128(2 * MARGIN + self.n1)
        self.start = ((1 << b) - 1) * WIDTH


GEO = [Geo(b) for b in range(4)]
SLOT_ROWS = 624
STEPS = (384, 640, 384, 256)


def place():
    return lax.axis_index("branch"), lax.axis_index("row"), lax.axis_index("col")


def per_branch(body):
    branch = place()[0]
    for g in GEO:

        @pl.when(branch == g.b)
        def _(g=g):
            body(g)


def cols_kernel(x, far, near, west, east):
    def body(g):
        for q in range(g.parts):
            for y in range(g.rows):
                lane = q * g.pixels + y * g.cols
                at = 2 * (q * g.rows + y)
                west[:, at : at + 2] = x[:, lane : lane + 2]
                last = lane + g.cols - 2
                east[:, at : at + 2] = x[:, last : last + 2]

    per_branch(body)
    odd = place()[2] % 2

    @pl.when(odd == 0)
    def _():
        far[...] = west[...]
        near[...] = east[...]

    @pl.when(odd == 1)
    def _():
        far[...] = east[...]
        near[...] = west[...]


def channel_order(g):
    out = lax.broadcasted_iota(jnp.int32, (g.channels, g.channels), 0)
    k = lax.broadcasted_iota(jnp.int32, (g.channels, g.channels), 1)
    part = jnp.zeros_like(k)
    for m in range(1, g.parts):
        part = part + (k >= WIDTH * m).astype(jnp.int32)
    at = (k - WIDTH * part) * g.parts + part
    return (at == out).astype(F32).astype(BF)


def side_places(g):
    n = lax.broadcasted_iota(jnp.int32, (1, g.padded), 1).astype(F32)
    y = jnp.floor((n + 0.5) * (1.0 / g.pitch))
    x = n - y * g.pitch
    right = x > g.cols + 1.0
    spot = 2.0 * y + jnp.where(right, x - (g.cols + 2.0) + 2.0 * g.rows, x)
    spot = jnp.where(((x < 2.0) | right) & (y < g.rows), spot, -1.0)
    k = lax.broadcasted_iota(jnp.int32, (g.sides, g.padded), 0).astype(F32)
    return (k == spot).astype(F32).astype(BF)


def prepare_kernel(x, _, *refs):
    xp_all, places, orders = refs[:4], refs[4:8], (None,) + refs[8:11]
    st_all = (x,) + refs[11:14]

    def body(g):
        c = g.channels
        st, xp = st_all[g.b], xp_all[g.b]
        places[g.b][...] = side_places(g)
        if g.b:
            order = channel_order(g)
            orders[g.b][...] = order
            for q in range(g.parts):
                st[q * WIDTH : (q + 1) * WIDTH, :] = x[:, q * g.pixels : (q + 1) * g.pixels]
            st[...] = nn(order, st[...]).astype(BF)
        xp[...] = jnp.zeros_like(xp)
        for y in range(g.rows):
            to = y * g.pitch + 2
            xp[:, to : to + g.cols] = st[:, y * g.cols : (y + 1) * g.cols]

    per_branch(body)


def runs(g, k):
    i = 0
    while i < g.high:
        y = (k * g.strip - 2 + i) % g.rows
        n = min(g.high - i, g.rows - y)
        yield i, y, n
        i += n


def strips_kernel(far, near, *refs):
    xp_all, places, orders, out = refs[:4], refs[4:8], (None,) + refs[8:11], refs[11]
    left, right = refs[12:14]
    st_all, xf_all, slot_all = refs[14:18], refs[18:22], refs[22:26]
    odd = place()[2] % 2

    @pl.when(odd == 0)
    def _():
        left[...] = far[...]
        right[...] = near[...]

    @pl.when(odd == 1)
    def _():
        left[...] = near[...]
        right[...] = far[...]

    def body(g):
        c, n = g.channels, 2 * g.rows
        st, xf, slot = st_all[g.b], xf_all[g.b], slot_all[g.b]
        for q in range(g.parts):
            for s, ref in enumerate((left, right)):
                st[q * WIDTH : (q + 1) * WIDTH, s * n : (s + 1) * n] = ref[:, q * n : (q + 1) * n]
        stacked = st[...]
        if g.b:
            stacked = nn(orders[g.b][...], stacked).astype(BF)
        xf[...] = xp_all[g.b][...] + nn(stacked, places[g.b][...]).astype(BF)
        for k in range(4):
            for i, y, rows in runs(g, k):
                at, lane, size = 1 + i * g.pitch, y * g.pitch, rows * g.pitch
                slot[:, at : at + size] = xf[:, lane : lane + size]
            for m in range(g.blocks):
                out[k, m * c : (m + 1) * c, :] = slot[:, 128 * m : 128 * (m + 1)]

    per_branch(body)


def inside(g, row_place, col_place):
    p = lax.broadcasted_iota(jnp.int32, (8, g.n1), 1).astype(F32)
    tile = jnp.floor((p + 0.5) * (1.0 / g.tile_h))
    rest = p - tile * g.tile_h
    row = jnp.floor((rest + 0.5) * (1.0 / g.pitch))
    x = rest - row * g.pitch
    y = row - 1.0 + (row_place * g.strip).astype(F32)
    out = (
        ((tile == 0.0) & (y < 0.0))
        | ((tile == 3.0) & (y > g.rows - 1.0))
        | ((x == 1.0) & (col_place == 0))
        | ((x == g.cols + 2.0) & (col_place == 15))
    )
    return jnp.where(out, 0.0, 1.0)[0:1, :]


def block_kernel(strips, bias, weight, out, *refs):
    wp_all, xs_all, col_all = refs[:4], refs[4:8], refs[8:12]
    hp_all, own_all = refs[12:16], refs[16:20]
    z0, zt_all = refs[20], (None,) + refs[21:24]
    wbuf, sems = refs[24:]
    _, row_place, col_place = place()

    def body(g):
        c = g.channels
        cl = up128(c)

        def fetch(layer, dy):
            return pltpu.make_async_copy(
                weight.at[0, layer, dy, :, 0:c, 0:cl],
                wbuf.at[layer, dy, :, 0:c, 0:cl],
                sems.at[layer, dy],
            )

        for layer in range(2):
            for dy in range(3):
                fetch(layer, dy).start()
        xs, hp, wp, col, own = xs_all[g.b], hp_all[g.b], wp_all[g.b], col_all[g.b], own_all[g.b]
        for tile in range(4):
            for m in range(g.blocks):
                xs[tile, :, 128 * m : 128 * (m + 1)] = strips[tile, m * c : (m + 1) * c, :]
        for i in range(g.high):
            lanes = slice(1 + i * g.pitch, 1 + (i + 1) * g.pitch)
            low = [k for k in range(4) if k * g.strip - 2 + i < 0]
            high = [k for k in range(4) if k * g.strip - 2 + i >= g.rows]
            if low:

                @pl.when(row_place <= max(low))
                def _(lanes=lanes):
                    for tile in (3, 2, 1):
                        xs[tile, :, lanes] = xs[tile - 1, :, lanes]
                    xs[0, :, lanes] = jnp.zeros((c, g.pitch), BF)

            if high:

                @pl.when(row_place >= min(high))
                def _(lanes=lanes):
                    for tile in (0, 1, 2):
                        xs[tile, :, lanes] = xs[tile + 1, :, lanes]
                    xs[3, :, lanes] = jnp.zeros((c, g.pitch), BF)

        for tile in range(4):
            lane = 1 + 2 * g.pitch
            own[:, tile * g.tile_z : (tile + 1) * g.tile_z] = xs[tile, :, lane : lane + g.tile_z]

        mask = inside(g, row_place, col_place)

        def column(layer):
            wide = jnp.broadcast_to(bias[0, layer : layer + 1, :], (8, 8 * WIDTH))
            return wide.T[0:c, 0:1]

        def conv(layer, view, size, n, finish):
            for dy in range(3):
                fetch(layer, dy).wait()
                for dx in range(3):
                    t = 3 * dy + dx
                    wp[:, c * t : c * (t + 1)] = wbuf[layer, dy, dx, 0:c, 0:c]
                    for tile in range(4):
                        col[c * t : c * (t + 1), tile * size : (tile + 1) * size] = view(
                            tile, dy * g.pitch + dx
                        )
            step = STEPS[g.b]
            for at in range(0, n, step):
                width = min(step, n - at)
                finish(at, width, nn(wp[...], col[:, at : at + width]))

        bias0 = column(0)

        def finish_first(at, size, total):
            h = jnp.maximum(total + bias0, 0.0) * mask[:, at : at + size]
            hp[:, MARGIN + at : MARGIN + at + size] = h.astype(BF)

        conv(0, lambda tile, lane: xs[tile, :, lane : lane + g.tile_h], g.tile_h, g.n1, finish_first)

        bias1 = column(1)

        def finish_second(at, size, total):
            z = jnp.maximum(total + bias1 + own[:, at : at + size].astype(F32), 0.0)
            if g.b == 0:
                z0[:, at : at + size] = z.astype(BF)
            else:
                zt_all[g.b][at : at + size, :] = z.T

        def hidden(tile, lane):
            lane += MARGIN + tile * g.tile_h - 1
            return hp[:, lane : lane + g.tile_z]

        conv(1, hidden, g.tile_z, g.n2, finish_second)

        for tile in range(4):
            for i in range(g.strip):
                at = tile * g.tile_z + i * g.pitch + 2
                if g.b == 0:
                    out[tile, i * WIDTH : (i + 1) * WIDTH, :] = z0[:, at : at + g.cols]
                    continue
                values = zt_all[g.b][at : at + g.cols, :].astype(BF)
                for m in range(cl // 128):
                    r = (m * g.strip + i) * g.cols
                    lanes = min(128, c - 128 * m)
                    out[tile, r : r + g.cols, 0:lanes] = values[:, 128 * m : 128 * m + lanes]

    per_branch(body)


def repeat_map(j, i):
    gj, gi = GEO[j], GEO[i]
    shape = (gj.pixels // 4, gi.pixels // 4)
    fine = lax.broadcasted_iota(jnp.int32, shape, 0)
    coarse = lax.broadcasted_iota(jnp.int32, shape, 1)
    return cover(fine, coarse, gj, i - j)


def cover(fine, coarse, g, d):
    bits = 7 - g.b
    y = fine >> bits
    x = fine & (g.cols - 1)
    return (((y >> d) << (bits - d)) + (x >> d) == coarse).astype(F32).astype(BF)


def repeat_map_t(j, i):
    gj, gi = GEO[j], GEO[i]
    shape = (gi.pixels // 4, gj.pixels // 4)
    coarse = lax.broadcasted_iota(jnp.int32, shape, 0)
    fine = lax.broadcasted_iota(jnp.int32, shape, 1)
    return cover(fine, coarse, gj, i - j)


def nn(a, b):
    return jnp.dot(a, b, preferred_element_type=F32)


def nt(a, b):
    return lax.dot_general(a, b, (((1,), (1,)), ((), ())), preferred_element_type=F32)


PAIRS = [(j, i) for j in range(4) for i in range(4) if i != j]
FINER = [(i, j) for i in range(4) for j in range(i + 1, 4)]


def maps_kernel(weight, _, *refs):
    blocks, shrink, grow = refs[:12], refs[12:18], refs[18:]
    for ref, (j, i) in zip(blocks, PAIRS):
        gj, gi = GEO[j], GEO[i]
        ref[...] = weight[gj.start : gj.start + gj.channels, gi.start : gi.start + gi.channels]
    for ref, (i, j) in zip(shrink, FINER):
        ref[...] = repeat_map_t(i, j)
    for ref, (i, j) in zip(grow, FINER[3:]):
        ref[...] = repeat_map(i, j)


def join_kernel(zb, bias, *refs):
    block = dict(zip(PAIRS, refs[:12]))
    shrink = dict(zip(FINER, refs[12:18]))
    grow = dict(zip(FINER[3:], refs[18:21]))
    out0, out1, out2, out3, z0s, s0 = refs[21:]
    for y in range(8):
        z0s[:, 128 * y : 128 * (y + 1)] = zb[0, WIDTH * y : WIDTH * (y + 1), :]
    z = [
        z0s[...],
        zb[1, 0:256, 0:96],
        jnp.concatenate([zb[2, 0:64, :], zb[2, 64:128, 0:64]], axis=1),
        jnp.concatenate([zb[3, 0:16, :], zb[3, 16:32, :], zb[3, 32:48, :]], axis=1),
    ]
    total = None
    for i in (1, 2, 3):
        term = nn(nt(block[0, i][...], z[i]).astype(BF), shrink[0, i][...])
        total = term if total is None else total + term
    wide = jnp.broadcast_to(bias[:, 0:WIDTH], (8, WIDTH))
    total = jnp.maximum(total + z[0].astype(F32) + wide.T[:, 0:1], 0.0)
    for y in range(8):
        s0[:, y, :] = total[:, 128 * y : 128 * (y + 1)]
    out0[...] = s0[...].astype(BF)

    for j, out in ((1, out1), (2, out2), (3, out3)):
        g = GEO[j]
        total = z[j].astype(F32) + bias[:, g.start : g.start + g.channels]
        for i in range(4):
            if i == j:
                continue
            if i < j:
                sums = (nt if i == 0 else nn)(shrink[i, j][...], z[i])
                mean = (sums * (0.25 ** (j - i))).astype(BF)
                total = total + nt(mean, block[j, i][...]).astype(BF).astype(F32)
            else:
                total = total + nn(grow[j, i][...], nt(z[i], block[j, i][...]).astype(BF))
        out[...] = jnp.maximum(total, 0.0).astype(BF)


def params(mib=32):
    return pltpu.CompilerParams(vmem_limit_bytes=mib * 1024 * 1024)


def like(*shapes):
    return tuple(jax.ShapeDtypeStruct(s, BF) for s in shapes)


def call_cols(x):
    return pl.pallas_call(
        cols_kernel,
        out_shape=like((WIDTH, 128), (WIDTH, 128)),
        in_specs=[VMEM],
        out_specs=(VMEM, VMEM),
        scratch_shapes=[pltpu.VMEM((WIDTH, 128), BF)] * 2,
        compiler_params=params(),
    )(x)


def call_prepare(x, after):
    shapes = [(g.channels, g.padded) for g in GEO]
    shapes += [(g.sides, g.padded) for g in GEO]
    shapes += [(g.channels, g.channels) for g in GEO[1:]]
    return pl.pallas_call(
        prepare_kernel,
        out_shape=like(*shapes),
        in_specs=[VMEM, pl.BlockSpec(memory_space=pl.ANY)],
        out_specs=(VMEM,) * len(shapes),
        scratch_shapes=[pltpu.VMEM((g.channels, g.pixels), BF) for g in GEO[1:]],
        compiler_params=params(),
        cost_estimate=pl.CostEstimate(flops=10**9, bytes_accessed=2**20, transcendentals=0),
    )(x, after)


def call_strips(far, near, padded):
    scratch = [pltpu.VMEM((WIDTH, 128), BF)] * 2
    scratch += [pltpu.VMEM((g.channels, g.sides), BF) for g in GEO]
    scratch += [pltpu.VMEM((g.channels, g.padded), BF) for g in GEO]
    scratch += [pltpu.VMEM((g.channels, g.slot), BF) for g in GEO]
    return pl.pallas_call(
        strips_kernel,
        out_shape=like((4, SLOT_ROWS, 128))[0],
        in_specs=[VMEM] * (2 + len(padded)),
        out_specs=VMEM,
        scratch_shapes=scratch,
        compiler_params=params(),
        cost_estimate=pl.CostEstimate(flops=10**10, bytes_accessed=2**24, transcendentals=0),
    )(far, near, *padded)


def call_block(strips, bias, weight):
    scratch = [pltpu.VMEM((g.channels, 9 * g.channels), BF) for g in GEO]
    scratch += [pltpu.VMEM((4, g.channels, g.slot), BF) for g in GEO]
    scratch += [pltpu.VMEM((9 * g.channels, g.n1), BF) for g in GEO]
    scratch += [pltpu.VMEM((g.channels, g.width_h), BF) for g in GEO]
    scratch += [pltpu.VMEM((g.channels, g.n2), BF) for g in GEO]
    scratch += [pltpu.VMEM((WIDTH, GEO[0].n2), BF)]
    scratch += [pltpu.VMEM((g.n2, g.channels), F32) for g in GEO[1:]]
    scratch += [pltpu.VMEM((2, 3, 3, 384, 384), BF), pltpu.SemaphoreType.DMA((2, 3))]
    return pl.pallas_call(
        block_kernel,
        out_shape=like((4, 384, 128))[0],
        in_specs=[VMEM, VMEM, pl.BlockSpec(memory_space=pltpu.HBM)],
        out_specs=VMEM,
        scratch_shapes=scratch,
        compiler_params=params(),
    )(strips, bias, weight)


def call_maps(weight, after):
    shapes = [(GEO[j].channels, GEO[i].channels) for j, i in PAIRS]
    shapes += [(GEO[j].pixels // 4, GEO[i].pixels // 4) for i, j in FINER]
    shapes += [(GEO[i].pixels // 4, GEO[j].pixels // 4) for i, j in FINER[3:]]
    return pl.pallas_call(
        maps_kernel,
        out_shape=like(*shapes),
        in_specs=[VMEM, pl.BlockSpec(memory_space=pl.ANY)],
        out_specs=(VMEM,) * len(shapes),
        compiler_params=params(),
        cost_estimate=pl.CostEstimate(flops=10**9, bytes_accessed=2**20, transcendentals=0),
    )(weight, after)


def call_join(received, bias, maps):
    return pl.pallas_call(
        join_kernel,
        out_shape=like((WIDTH, 8, 128), (256, 96), (64, 192), (16, 384)),
        in_specs=[VMEM] * (2 + len(maps)),
        out_specs=(VMEM,) * 4,
        scratch_shapes=[
            pltpu.VMEM((WIDTH, 1024), BF),
            pltpu.VMEM((WIDTH, 8, 128), F32),
        ],
        compiler_params=params(),
    )(received, bias, *maps)


def paired(shard, first):
    size = lax.axis_size("col")
    pairs = []
    for c in range(first, size - 1, 2):
        pairs += [(c, c + 1), (c + 1, c)]
    return lax.ppermute(shard, "col", pairs)


def swapped(parts, axis):
    return lax.all_to_all(parts, axis, split_axis=0, concat_axis=0, tiled=True)


def local(section_in, conv_weight, conv_bias, join_weight, join_bias):
    x = section_in[0, 0, 0]
    far, near = call_cols(x)
    padded = call_prepare(x, far)
    strips = call_strips(paired(far, 1), paired(near, 0), padded)
    settled = call_block(swapped(strips, "row"), conv_bias, conv_weight)
    maps = call_maps(join_weight, settled)
    out = call_join(swapped(settled, "branch"), join_bias[None, :], maps)
    first = [out[0]]
    for g in GEO[1:]:
        pixel_major = out[g.b].reshape(g.strip, g.cols, g.channels)
        first.append(pixel_major.transpose(2, 0, 1))
    return tuple(first)


def solution(mesh):
    in_specs = (
        P("branch", "row", "col", None, None),
        P("branch", None, None, None, None, None),
        P("branch", None, None),
        P(),
        P(),
    )
    out_specs = (P(None, ("branch", "row"), "col"),) * 4
    return jax.shard_map(local, mesh=mesh, in_specs=in_specs, out_specs=out_specs, check_vma=False)
```

```python
import jax
import jax.numpy as jnp
from jax import lax
from jax.experimental import pallas as pl
from jax.experimental.pallas import tpu as pltpu
from jax.sharding import PartitionSpec as P

WIDTH = 48
TH = 32
TW = 128
BF = jnp.bfloat16
F32 = jnp.float32
VMEM = pl.BlockSpec(memory_space=pltpu.VMEM)


def up128(n):
    return -(-n // 128) * 128


class Geo:
    def __init__(self, b):
        self.b = b
        self.parts = 1 << b
        self.channels = WIDTH << b
        self.rows = TH >> b
        self.cols = TW >> b
        self.pixels = self.rows * self.cols
        self.strip = self.rows // 4
        self.high = self.strip + 4
        self.pitch = self.cols + 4
        self.padded = up128(self.rows * self.pitch)
        self.sides = 4 * self.rows
        self.slot = up128(self.high * self.pitch)
        self.blocks = self.slot // 128
        self.wide = up128(4 * self.pitch)
        self.lanes = self.high * self.wide
        self.n1 = (self.strip + 2) * self.wide
        self.n2 = self.strip * self.wide
        self.start = ((1 << b) - 1) * WIDTH


GEO = [Geo(b) for b in range(4)]
SLOT_ROWS = 624
STEPS = (640, 768, 512, 384)


def place():
    return lax.axis_index("branch"), lax.axis_index("row"), lax.axis_index("col")


def per_branch(body):
    branch = place()[0]
    for g in GEO:

        @pl.when(branch == g.b)
        def _(g=g):
            body(g)


def cols_kernel(x, far, near, west, east):
    def body(g):
        for q in range(g.parts):
            for y in range(g.rows):
                lane = q * g.pixels + y * g.cols
                at = 2 * (q * g.rows + y)
                west[:, at : at + 2] = x[:, lane : lane + 2]
                last = lane + g.cols - 2
                east[:, at : at + 2] = x[:, last : last + 2]

    per_branch(body)
    odd = place()[2] % 2

    @pl.when(odd == 0)
    def _():
        far[...] = west[...]
        near[...] = east[...]

    @pl.when(odd == 1)
    def _():
        far[...] = east[...]
        near[...] = west[...]


def channel_order(g):
    out = lax.broadcasted_iota(jnp.int32, (g.channels, g.channels), 0)
    k = lax.broadcasted_iota(jnp.int32, (g.channels, g.channels), 1)
    part = jnp.zeros_like(k)
    for m in range(1, g.parts):
        part = part + (k >= WIDTH * m).astype(jnp.int32)
    at = (k - WIDTH * part) * g.parts + part
    return (at == out).astype(F32).astype(BF)


def side_places(g):
    n = lax.broadcasted_iota(jnp.int32, (1, g.padded), 1).astype(F32)
    y = jnp.floor((n + 0.5) * (1.0 / g.pitch))
    x = n - y * g.pitch
    right = x > g.cols + 1.0
    spot = 2.0 * y + jnp.where(right, x - (g.cols + 2.0) + 2.0 * g.rows, x)
    spot = jnp.where(((x < 2.0) | right) & (y < g.rows), spot, -1.0)
    k = lax.broadcasted_iota(jnp.int32, (g.sides, g.padded), 0).astype(F32)
    return (k == spot).astype(F32).astype(BF)


def prepare_kernel(x, weight, _, *refs):
    xp_all, wp_all, places, orders = refs[:4], refs[4:8], refs[8:12], (None,) + refs[12:15]
    st_all = (x,) + refs[15:18]

    def body(g):
        c = g.channels
        st, xp, wp = st_all[g.b], xp_all[g.b], wp_all[g.b]
        places[g.b][...] = side_places(g)
        if g.b:
            order = channel_order(g)
            orders[g.b][...] = order
            for q in range(g.parts):
                st[q * WIDTH : (q + 1) * WIDTH, :] = x[:, q * g.pixels : (q + 1) * g.pixels]
            st[...] = nn(order, st[...]).astype(BF)
        xp[...] = jnp.zeros_like(xp)
        for y in range(g.rows):
            to = y * g.pitch + 2
            xp[:, to : to + g.cols] = st[:, y * g.cols : (y + 1) * g.cols]
        for layer in range(2):
            for dy in range(3):
                for dx in range(3):
                    tap = weight[0, layer, dy, dx, 0:c, 0:c]
                    wp[layer, dy, :, c * dx : c * (dx + 1)] = tap

    per_branch(body)


def runs(g, k):
    i = 0
    while i < g.high:
        y = (k * g.strip - 2 + i) % g.rows
        n = min(g.high - i, g.rows - y)
        yield i, y, n
        i += n


def strips_kernel(far, near, *refs):
    xp_all, places, orders, out = refs[:4], refs[4:8], (None,) + refs[8:11], refs[11]
    left, right = refs[12:14]
    st_all, xf_all, slot_all = refs[14:18], refs[18:22], refs[22:26]
    odd = place()[2] % 2

    @pl.when(odd == 0)
    def _():
        left[...] = far[...]
        right[...] = near[...]

    @pl.when(odd == 1)
    def _():
        left[...] = near[...]
        right[...] = far[...]

    def body(g):
        c, n = g.channels, 2 * g.rows
        st, xf, slot = st_all[g.b], xf_all[g.b], slot_all[g.b]
        for q in range(g.parts):
            for s, ref in enumerate((left, right)):
                st[q * WIDTH : (q + 1) * WIDTH, s * n : (s + 1) * n] = ref[:, q * n : (q + 1) * n]
        stacked = st[...]
        if g.b:
            stacked = nn(orders[g.b][...], stacked).astype(BF)
        xf[...] = xp_all[g.b][...] + nn(stacked, places[g.b][...]).astype(BF)
        for k in range(4):
            for i, y, rows in runs(g, k):
                at, lane, size = i * g.pitch, y * g.pitch, rows * g.pitch
                slot[:, at : at + size] = xf[:, lane : lane + size]
            for m in range(g.blocks):
                out[k, m * c : (m + 1) * c, :] = slot[:, 128 * m : 128 * (m + 1)]

    per_branch(body)


def inside(g, row_place, col_place):
    p = lax.broadcasted_iota(jnp.int32, (8, g.n1), 1).astype(F32)
    row = jnp.floor((p + 0.5) * (1.0 / g.wide))
    rest = p - row * g.wide
    tile = jnp.floor((rest + 0.5) * (1.0 / g.pitch))
    x = rest - tile * g.pitch
    y = row - 1.0 + (row_place * g.strip).astype(F32)
    out = (
        ((tile == 0.0) & (y < 0.0))
        | ((tile == 3.0) & (y > g.rows - 1.0))
        | ((x == 1.0) & (col_place == 0))
        | ((x == g.cols + 2.0) & (col_place == 15))
    )
    return jnp.where(out, 0.0, 1.0)[0:1, :]


def block_kernel(strips, bias, *refs):
    wp_all, out = refs[:4], refs[4]
    xr_all, hr_all, z0, zt_all = refs[5:9], refs[9:13], refs[13], (None,) + refs[14:17]
    _, row_place, col_place = place()

    def body(g):
        c = g.channels
        cl = up128(c)
        xr, hr, wp = xr_all[g.b], hr_all[g.b], wp_all[g.b]

        def put(i, tile, source):
            lane, to, left = i * g.pitch, i * g.wide + tile * g.pitch, g.pitch
            while left:
                m, at = divmod(lane, 128)
                n = min(left, 128 - at)
                if 0 <= source < 4:
                    piece = strips[source, m * c : (m + 1) * c, at : at + n]
                else:
                    piece = jnp.zeros((c, n), BF)
                xr[c : 2 * c, to : to + n] = piece
                lane, to, left = lane + n, to + n, left - n

        for i in range(g.high):
            low = [k for k in range(4) if k * g.strip - 2 + i < 0]
            high = [k for k in range(4) if k * g.strip - 2 + i >= g.rows]
            for tile in range(4):
                put(i, tile, tile)
            if low:

                @pl.when(row_place <= max(low))
                def _(i=i):
                    for tile in range(4):
                        put(i, tile, tile - 1)

            if high:

                @pl.when(row_place >= min(high))
                def _(i=i):
                    for tile in range(4):
                        put(i, tile, tile + 1)

        mask = inside(g, row_place, col_place)

        def column(layer):
            wide = jnp.broadcast_to(bias[0, layer : layer + 1, :], (8, 8 * WIDTH))
            return wide.T[0:c, 0:1]

        def conv(layer, maps, size, n, finish):
            maps[0:c, 1:size] = maps[c : 2 * c, 0 : size - 1]
            maps[2 * c : 3 * c, 0 : size - 1] = maps[c : 2 * c, 1:size]
            step = STEPS[g.b]
            for at in range(0, n, step):
                width = min(step, n - at)
                total = None
                for dy in range(3):
                    lane = at + dy * g.wide
                    term = nn(wp[layer, dy], maps[:, lane : lane + width])
                    total = term if total is None else total + term
                finish(at, width, total)

        bias0 = column(0)

        def finish_first(at, size, total):
            h = jnp.maximum(total + bias0, 0.0) * mask[:, at : at + size]
            hr[c : 2 * c, at : at + size] = h.astype(BF)

        conv(0, xr, g.lanes, g.n1, finish_first)

        bias1 = column(1)

        def finish_second(at, size, total):
            lane = 2 * g.wide + at
            z = jnp.maximum(total + bias1 + xr[c : 2 * c, lane : lane + size].astype(F32), 0.0)
            if g.b == 0:
                z0[:, at : at + size] = z.astype(BF)
            else:
                zt_all[g.b][at : at + size, :] = z.T

        conv(1, hr, g.n1, g.n2, finish_second)

        for tile in range(4):
            for i in range(g.strip):
                at = i * g.wide + tile * g.pitch + 2
                if g.b == 0:
                    out[tile, i * WIDTH : (i + 1) * WIDTH, :] = z0[:, at : at + g.cols]
                    continue
                values = zt_all[g.b][at : at + g.cols, :].astype(BF)
                for m in range(cl // 128):
                    r = (m * g.strip + i) * g.cols
                    lanes = min(128, c - 128 * m)
                    out[tile, r : r + g.cols, 0:lanes] = values[:, 128 * m : 128 * m + lanes]

    per_branch(body)


def repeat_map(j, i):
    gj, gi = GEO[j], GEO[i]
    shape = (gj.pixels // 4, gi.pixels // 4)
    fine = lax.broadcasted_iota(jnp.int32, shape, 0)
    coarse = lax.broadcasted_iota(jnp.int32, shape, 1)
    return cover(fine, coarse, gj, i - j)


def cover(fine, coarse, g, d):
    bits = 7 - g.b
    y = fine >> bits
    x = fine & (g.cols - 1)
    return (((y >> d) << (bits - d)) + (x >> d) == coarse).astype(F32).astype(BF)


def repeat_map_t(j, i):
    gj, gi = GEO[j], GEO[i]
    shape = (gi.pixels // 4, gj.pixels // 4)
    coarse = lax.broadcasted_iota(jnp.int32, shape, 0)
    fine = lax.broadcasted_iota(jnp.int32, shape, 1)
    return cover(fine, coarse, gj, i - j)


def nn(a, b):
    return jnp.dot(a, b, preferred_element_type=F32)


def nt(a, b):
    return lax.dot_general(a, b, (((1,), (1,)), ((), ())), preferred_element_type=F32)


def join_kernel(zb, weight, bias, out0, out1, out2, out3, z0s, s0):
    for y in range(8):
        z0s[:, 128 * y : 128 * (y + 1)] = zb[0, WIDTH * y : WIDTH * (y + 1), :]
    z = [
        z0s[...],
        zb[1, 0:256, 0:96],
        jnp.concatenate([zb[2, 0:64, :], zb[2, 64:128, 0:64]], axis=1),
        jnp.concatenate([zb[3, 0:16, :], zb[3, 16:32, :], zb[3, 32:48, :]], axis=1),
    ]

    def block(j, i):
        gj, gi = GEO[j], GEO[i]
        return weight[gj.start : gj.start + gj.channels, gi.start : gi.start + gi.channels]

    total = None
    for i in (1, 2, 3):
        term = nn(nt(block(0, i), z[i]).astype(BF), repeat_map_t(0, i))
        total = term if total is None else total + term
    wide = jnp.broadcast_to(bias[:, 0:WIDTH], (8, WIDTH))
    total = jnp.maximum(total + z[0].astype(F32) + wide.T[:, 0:1], 0.0)
    for y in range(8):
        s0[:, y, :] = total[:, 128 * y : 128 * (y + 1)]
    out0[...] = s0[...].astype(BF)

    for j, out in ((1, out1), (2, out2), (3, out3)):
        g = GEO[j]
        total = z[j].astype(F32) + bias[:, g.start : g.start + g.channels]
        for i in range(4):
            if i == j:
                continue
            if i < j:
                sums = (nt if i == 0 else nn)(repeat_map_t(i, j), z[i])
                mean = (sums * (0.25 ** (j - i))).astype(BF)
                total = total + nt(mean, block(j, i)).astype(BF).astype(F32)
            else:
                total = total + nn(repeat_map(j, i), nt(z[i], block(j, i)).astype(BF))
        out[...] = jnp.maximum(total, 0.0).astype(BF)


def params(mib=24):
    return pltpu.CompilerParams(vmem_limit_bytes=mib * 1024 * 1024)


def like(*shapes):
    return tuple(jax.ShapeDtypeStruct(s, BF) for s in shapes)


def call_cols(x):
    return pl.pallas_call(
        cols_kernel,
        out_shape=like((WIDTH, 128), (WIDTH, 128)),
        in_specs=[VMEM],
        out_specs=(VMEM, VMEM),
        scratch_shapes=[pltpu.VMEM((WIDTH, 128), BF)] * 2,
        compiler_params=params(),
    )(x)


def call_prepare(x, weight, after):
    shapes = [(g.channels, g.padded) for g in GEO]
    shapes += [(2, 3, g.channels, 3 * g.channels) for g in GEO]
    shapes += [(g.sides, g.padded) for g in GEO]
    shapes += [(g.channels, g.channels) for g in GEO[1:]]
    made = pl.pallas_call(
        prepare_kernel,
        out_shape=like(*shapes),
        in_specs=[VMEM, VMEM, pl.BlockSpec(memory_space=pl.ANY)],
        out_specs=(VMEM,) * len(shapes),
        scratch_shapes=[pltpu.VMEM((g.channels, g.pixels), BF) for g in GEO[1:]],
        compiler_params=params(),
        cost_estimate=pl.CostEstimate(flops=10**9, bytes_accessed=12 * 2**20, transcendentals=0),
    )(x, weight, after)
    return made[:4] + made[8:], made[4:8]


def call_strips(far, near, padded):
    scratch = [pltpu.VMEM((WIDTH, 128), BF)] * 2
    scratch += [pltpu.VMEM((g.channels, g.sides), BF) for g in GEO]
    scratch += [pltpu.VMEM((g.channels, g.padded), BF) for g in GEO]
    scratch += [pltpu.VMEM((g.channels, g.slot), BF) for g in GEO]
    return pl.pallas_call(
        strips_kernel,
        out_shape=like((4, SLOT_ROWS, 128))[0],
        in_specs=[VMEM] * (2 + len(padded)),
        out_specs=VMEM,
        scratch_shapes=scratch,
        compiler_params=params(),
    )(far, near, *padded)


def call_block(strips, bias, weights):
    scratch = [pltpu.VMEM((3 * g.channels, g.lanes), BF) for g in GEO]
    scratch += [pltpu.VMEM((3 * g.channels, g.n1), BF) for g in GEO]
    scratch += [pltpu.VMEM((WIDTH, GEO[0].n2), BF)]
    scratch += [pltpu.VMEM((g.n2, g.channels), F32) for g in GEO[1:]]
    return pl.pallas_call(
        block_kernel,
        out_shape=like((4, 384, 128))[0],
        in_specs=[VMEM] * 6,
        out_specs=VMEM,
        scratch_shapes=scratch,
        compiler_params=params(),
    )(strips, bias, *weights)


def call_join(received, weight, bias):
    return pl.pallas_call(
        join_kernel,
        out_shape=like((WIDTH, 8, 128), (256, 96), (64, 192), (16, 384)),
        in_specs=[VMEM] * 3,
        out_specs=(VMEM,) * 4,
        scratch_shapes=[
            pltpu.VMEM((WIDTH, 1024), BF),
            pltpu.VMEM((WIDTH, 8, 128), F32),
        ],
        compiler_params=params(),
    )(received, weight, bias)


def paired(shard, first):
    size = lax.axis_size("col")
    pairs = []
    for c in range(first, size - 1, 2):
        pairs += [(c, c + 1), (c + 1, c)]
    return lax.ppermute(shard, "col", pairs)


def swapped(parts, axis):
    return lax.all_to_all(parts, axis, split_axis=0, concat_axis=0, tiled=True)


def local(section_in, conv_weight, conv_bias, join_weight, join_bias):
    x = section_in[0, 0, 0]
    far, near = call_cols(x)
    padded, weights = call_prepare(x, conv_weight, far)
    strips = call_strips(paired(far, 1), paired(near, 0), padded)
    settled = call_block(swapped(strips, "row"), conv_bias, weights)
    out = call_join(swapped(settled, "branch"), join_weight, join_bias[None, :])
    first = [out[0]]
    for g in GEO[1:]:
        pixel_major = out[g.b].reshape(g.strip, g.cols, g.channels)
        first.append(pixel_major.transpose(2, 0, 1))
    return tuple(first)


def solution(mesh):
    in_specs = (
        P("branch", "row", "col", None, None),
        P("branch", None, None, None, None, None),
        P("branch", None, None),
        P(),
        P(),
    )
    out_specs = (P(None, ("branch", "row"), "col"),) * 4
    return jax.shard_map(local, mesh=mesh, in_specs=in_specs, out_specs=out_specs, check_vma=False)
```

```python
import jax
import jax.numpy as jnp
from jax import lax
from jax.experimental import pallas as pl
from jax.experimental.pallas import tpu as pltpu
from jax.sharding import PartitionSpec as P

WIDTH = 48
TH = 32
TW = 128
BF = jnp.bfloat16
F32 = jnp.float32
VMEM = pl.BlockSpec(memory_space=pltpu.VMEM)


def up128(n):
    return -(-n // 128) * 128


class Geo:
    def __init__(self, b):
        self.b = b
        self.parts = 1 << b
        self.channels = WIDTH << b
        self.rows = TH >> b
        self.cols = TW >> b
        self.pixels = self.rows * self.cols
        self.strip = self.rows // 4
        self.high = self.strip + 4
        self.pitch = self.cols + 4
        self.padded = up128(self.rows * self.pitch)
        self.sides = 4 * self.rows
        self.slot = up128(self.high * self.pitch)
        self.blocks = self.slot // 128
        self.wide = up128(4 * self.pitch)
        self.lanes = self.high * self.wide
        self.n1 = (self.strip + 2) * self.wide
        self.n2 = self.strip * self.wide
        self.start = ((1 << b) - 1) * WIDTH


GEO = [Geo(b) for b in range(4)]
SLOT_ROWS = 624
STEPS = (640, 768, 512, 384)


def place():
    return lax.axis_index("branch"), lax.axis_index("row"), lax.axis_index("col")


def per_branch(body):
    branch = place()[0]
    for g in GEO:

        @pl.when(branch == g.b)
        def _(g=g):
            body(g)


def cols_kernel(x, far, near, west, east):
    def body(g):
        for q in range(g.parts):
            for y in range(g.rows):
                lane = q * g.pixels + y * g.cols
                at = 2 * (q * g.rows + y)
                west[:, at : at + 2] = x[:, lane : lane + 2]
                last = lane + g.cols - 2
                east[:, at : at + 2] = x[:, last : last + 2]

    per_branch(body)
    odd = place()[2] % 2

    @pl.when(odd == 0)
    def _():
        far[...] = west[...]
        near[...] = east[...]

    @pl.when(odd == 1)
    def _():
        far[...] = east[...]
        near[...] = west[...]


def channel_order(g):
    out = lax.broadcasted_iota(jnp.int32, (g.channels, g.channels), 0)
    k = lax.broadcasted_iota(jnp.int32, (g.channels, g.channels), 1)
    part = jnp.zeros_like(k)
    for m in range(1, g.parts):
        part = part + (k >= WIDTH * m).astype(jnp.int32)
    at = (k - WIDTH * part) * g.parts + part
    return (at == out).astype(F32).astype(BF)


def side_places(g):
    n = lax.broadcasted_iota(jnp.int32, (1, g.padded), 1).astype(F32)
    y = jnp.floor((n + 0.5) * (1.0 / g.pitch))
    x = n - y * g.pitch
    right = x > g.cols + 1.0
    spot = 2.0 * y + jnp.where(right, x - (g.cols + 2.0) + 2.0 * g.rows, x)
    spot = jnp.where(((x < 2.0) | right) & (y < g.rows), spot, -1.0)
    k = lax.broadcasted_iota(jnp.int32, (g.sides, g.padded), 0).astype(F32)
    return (k == spot).astype(F32).astype(BF)


def prepare_kernel(x_hbm, weight, _, *refs):
    xp_all, wp_all, places, orders = refs[:4], refs[4:8], refs[8:12], (None,) + refs[12:15]
    wbuf, sems, x, x_sem = refs[18:]
    st_all = (x,) + refs[15:18]
    copy = pltpu.make_async_copy(x_hbm, x, x_sem)
    copy.start()

    def body(g):
        c = g.channels
        st, xp, wp = st_all[g.b], xp_all[g.b], wp_all[g.b]
        cl = up128(c)

        def fetch(layer):
            return pltpu.make_async_copy(
                weight.at[0, layer, :, :, 0:c, 0:cl],
                wbuf.at[layer, :, :, 0:c, 0:cl],
                sems.at[layer],
            )

        fetch(0).start()
        fetch(1).start()
        places[g.b][...] = side_places(g)
        if g.b:
            order = channel_order(g)
            orders[g.b][...] = order
        xp[...] = jnp.zeros_like(xp)
        copy.wait()
        if g.b:
            for q in range(g.parts):
                st[q * WIDTH : (q + 1) * WIDTH, :] = x[:, q * g.pixels : (q + 1) * g.pixels]
            st[...] = nn(order, st[...]).astype(BF)
        for y in range(g.rows):
            to = y * g.pitch + 2
            xp[:, to : to + g.cols] = st[:, y * g.cols : (y + 1) * g.cols]
        for layer in range(2):
            fetch(layer).wait()
            for dy in range(3):
                for dx in range(3):
                    tap = wbuf[layer, dy, dx, 0:c, 0:c]
                    wp[layer, dy, :, c * dx : c * (dx + 1)] = tap

    per_branch(body)


def runs(g, k):
    i = 0
    while i < g.high:
        y = (k * g.strip - 2 + i) % g.rows
        n = min(g.high - i, g.rows - y)
        yield i, y, n
        i += n


def strips_kernel(far, near, *refs):
    xp_all, places, orders, out = refs[:4], refs[4:8], (None,) + refs[8:11], refs[11]
    left, right = refs[12:14]
    st_all, xf_all, slot_all = refs[14:18], refs[18:22], refs[22:26]
    odd = place()[2] % 2

    @pl.when(odd == 0)
    def _():
        left[...] = far[...]
        right[...] = near[...]

    @pl.when(odd == 1)
    def _():
        left[...] = near[...]
        right[...] = far[...]

    def body(g):
        c, n = g.channels, 2 * g.rows
        st, xf, slot = st_all[g.b], xf_all[g.b], slot_all[g.b]
        for q in range(g.parts):
            for s, ref in enumerate((left, right)):
                st[q * WIDTH : (q + 1) * WIDTH, s * n : (s + 1) * n] = ref[:, q * n : (q + 1) * n]
        stacked = st[...]
        if g.b:
            stacked = nn(orders[g.b][...], stacked).astype(BF)
        xf[...] = xp_all[g.b][...] + nn(stacked, places[g.b][...]).astype(BF)
        for k in range(4):
            for i, y, rows in runs(g, k):
                at, lane, size = i * g.pitch, y * g.pitch, rows * g.pitch
                slot[:, at : at + size] = xf[:, lane : lane + size]
            for m in range(g.blocks):
                out[k, m * c : (m + 1) * c, :] = slot[:, 128 * m : 128 * (m + 1)]

    per_branch(body)


def inside(g, row_place, col_place):
    p = lax.broadcasted_iota(jnp.int32, (8, g.n1), 1).astype(F32)
    row = jnp.floor((p + 0.5) * (1.0 / g.wide))
    rest = p - row * g.wide
    tile = jnp.floor((rest + 0.5) * (1.0 / g.pitch))
    x = rest - tile * g.pitch
    y = row - 1.0 + (row_place * g.strip).astype(F32)
    out = (
        ((tile == 0.0) & (y < 0.0))
        | ((tile == 3.0) & (y > g.rows - 1.0))
        | ((x == 1.0) & (col_place == 0))
        | ((x == g.cols + 2.0) & (col_place == 15))
    )
    return jnp.where(out, 0.0, 1.0)[0:1, :]


def block_kernel(strips, bias, *refs):
    wp_all, out = refs[:4], refs[4]
    xr_all, hr_all, z0, zt_all = refs[5:9], refs[9:13], refs[13], (None,) + refs[14:17]
    _, row_place, col_place = place()

    def body(g):
        c = g.channels
        cl = up128(c)
        xr, hr, wp = xr_all[g.b], hr_all[g.b], wp_all[g.b]

        def put(i, tile, source):
            lane, to, left = i * g.pitch, i * g.wide + tile * g.pitch, g.pitch
            while left:
                m, at = divmod(lane, 128)
                n = min(left, 128 - at)
                if 0 <= source < 4:
                    piece = strips[source, m * c : (m + 1) * c, at : at + n]
                else:
                    piece = jnp.zeros((c, n), BF)
                xr[c : 2 * c, to : to + n] = piece
                lane, to, left = lane + n, to + n, left - n

        for i in range(g.high):
            low = [k for k in range(4) if k * g.strip - 2 + i < 0]
            high = [k for k in range(4) if k * g.strip - 2 + i >= g.rows]
            for tile in range(4):
                put(i, tile, tile)
            if low:

                @pl.when(row_place <= max(low))
                def _(i=i):
                    for tile in range(4):
                        put(i, tile, tile - 1)

            if high:

                @pl.when(row_place >= min(high))
                def _(i=i):
                    for tile in range(4):
                        put(i, tile, tile + 1)

        mask = inside(g, row_place, col_place)

        def column(layer):
            wide = jnp.broadcast_to(bias[0, layer : layer + 1, :], (8, 8 * WIDTH))
            return wide.T[0:c, 0:1]

        def conv(layer, maps, size, n, finish):
            maps[0:c, 1:size] = maps[c : 2 * c, 0 : size - 1]
            maps[2 * c : 3 * c, 0 : size - 1] = maps[c : 2 * c, 1:size]
            step = STEPS[g.b]
            for at in range(0, n, step):
                width = min(step, n - at)
                total = None
                for dy in range(3):
                    lane = at + dy * g.wide
                    term = nn(wp[layer, dy], maps[:, lane : lane + width])
                    total = term if total is None else total + term
                finish(at, width, total)

        bias0 = column(0)

        def finish_first(at, size, total):
            h = jnp.maximum(total + bias0, 0.0) * mask[:, at : at + size]
            hr[c : 2 * c, at : at + size] = h.astype(BF)

        conv(0, xr, g.lanes, g.n1, finish_first)

        bias1 = column(1)

        def finish_second(at, size, total):
            lane = 2 * g.wide + at
            z = jnp.maximum(total + bias1 + xr[c : 2 * c, lane : lane + size].astype(F32), 0.0)
            if g.b == 0:
                z0[:, at : at + size] = z.astype(BF)
            else:
                zt_all[g.b][at : at + size, :] = z.T

        conv(1, hr, g.n1, g.n2, finish_second)

        for tile in range(4):
            for i in range(g.strip):
                at = i * g.wide + tile * g.pitch + 2
                if g.b == 0:
                    out[tile, i * WIDTH : (i + 1) * WIDTH, :] = z0[:, at : at + g.cols]
                    continue
                values = zt_all[g.b][at : at + g.cols, :].astype(BF)
                for m in range(cl // 128):
                    r = (m * g.strip + i) * g.cols
                    lanes = min(128, c - 128 * m)
                    out[tile, r : r + g.cols, 0:lanes] = values[:, 128 * m : 128 * m + lanes]

    per_branch(body)


def repeat_map(j, i):
    gj, gi = GEO[j], GEO[i]
    shape = (gj.pixels // 4, gi.pixels // 4)
    fine = lax.broadcasted_iota(jnp.int32, shape, 0)
    coarse = lax.broadcasted_iota(jnp.int32, shape, 1)
    return cover(fine, coarse, gj, i - j)


def cover(fine, coarse, g, d):
    bits = 7 - g.b
    y = fine >> bits
    x = fine & (g.cols - 1)
    return (((y >> d) << (bits - d)) + (x >> d) == coarse).astype(F32).astype(BF)


def repeat_map_t(j, i):
    gj, gi = GEO[j], GEO[i]
    shape = (gi.pixels // 4, gj.pixels // 4)
    coarse = lax.broadcasted_iota(jnp.int32, shape, 0)
    fine = lax.broadcasted_iota(jnp.int32, shape, 1)
    return cover(fine, coarse, gj, i - j)


def nn(a, b):
    return jnp.dot(a, b, preferred_element_type=F32)


def nt(a, b):
    return lax.dot_general(a, b, (((1,), (1,)), ((), ())), preferred_element_type=F32)


def join_kernel(zb, weight, bias, out0, out1, out2, out3, z0s, s0):
    for y in range(8):
        z0s[:, 128 * y : 128 * (y + 1)] = zb[0, WIDTH * y : WIDTH * (y + 1), :]
    z = [
        z0s[...],
        zb[1, 0:256, 0:96],
        jnp.concatenate([zb[2, 0:64, :], zb[2, 64:128, 0:64]], axis=1),
        jnp.concatenate([zb[3, 0:16, :], zb[3, 16:32, :], zb[3, 32:48, :]], axis=1),
    ]

    def block(j, i, last=None):
        first, end = GEO[j], GEO[j if last is None else last]
        gi = GEO[i]
        rows = slice(first.start, end.start + end.channels)
        return weight[rows, gi.start : gi.start + gi.channels]

    def tn(a, b):
        return lax.dot_general(a, b, (((0,), (0,)), ((), ())), preferred_element_type=F32)

    size = [g.pixels // 4 for g in GEO]
    terms = {i: nt(z[i], block(0, i, i - 1)).astype(BF) for i in (1, 2, 3)}
    shrink0 = jnp.concatenate([repeat_map_t(0, i) for i in (1, 2, 3)], axis=0)
    shrink1 = jnp.concatenate([repeat_map_t(1, i) for i in (2, 3)], axis=0)
    sums = {0: nt(shrink0, z[0]), 1: nn(shrink1, z[1]), 2: nn(repeat_map_t(2, 3), z[2])}

    stacked = jnp.concatenate([terms[i][:, 0:WIDTH] for i in (1, 2, 3)], axis=0)
    wide = jnp.broadcast_to(bias[:, 0:WIDTH], (8, WIDTH))
    total = tn(stacked, shrink0) + z[0].astype(F32) + wide.T[:, 0:1]
    total = jnp.maximum(total, 0.0)
    for y in range(8):
        s0[:, y, :] = total[:, 128 * y : 128 * (y + 1)]
    out0[...] = s0[...].astype(BF)

    for j, out in ((1, out1), (2, out2), (3, out3)):
        g = GEO[j]
        total = z[j].astype(F32) + bias[:, g.start : g.start + g.channels]
        for i in range(j):
            first = sum(size[i + 1 : j])
            mean = (sums[i][first : first + size[j], :] * (0.25 ** (j - i))).astype(BF)
            total = total + nt(mean, block(j, i)).astype(BF).astype(F32)
        for i in range(j + 1, 4):
            term = terms[i][:, g.start : g.start + g.channels]
            total = total + nn(repeat_map(j, i), term)
        out[...] = jnp.maximum(total, 0.0).astype(BF)


def params(mib=24):
    return pltpu.CompilerParams(vmem_limit_bytes=mib * 1024 * 1024)


def like(*shapes):
    return tuple(jax.ShapeDtypeStruct(s, BF) for s in shapes)


def call_cols(x):
    return pl.pallas_call(
        cols_kernel,
        out_shape=like((WIDTH, 128), (WIDTH, 128)),
        in_specs=[VMEM],
        out_specs=(VMEM, VMEM),
        scratch_shapes=[pltpu.VMEM((WIDTH, 128), BF)] * 2,
        compiler_params=params(),
    )(x)


def call_prepare(x, weight, after):
    shapes = [(g.channels, g.padded) for g in GEO]
    shapes += [(2, 3, g.channels, 3 * g.channels) for g in GEO]
    shapes += [(g.sides, g.padded) for g in GEO]
    shapes += [(g.channels, g.channels) for g in GEO[1:]]
    made = pl.pallas_call(
        prepare_kernel,
        out_shape=like(*shapes),
        in_specs=[pl.BlockSpec(memory_space=pltpu.HBM)] * 2 + [pl.BlockSpec(memory_space=pl.ANY)],
        out_specs=(VMEM,) * len(shapes),
        scratch_shapes=[pltpu.VMEM((g.channels, g.pixels), BF) for g in GEO[1:]]
        + [pltpu.VMEM((2, 3, 3, 384, 384), BF), pltpu.SemaphoreType.DMA((2,))]
        + [pltpu.VMEM((WIDTH, TH * TW), BF), pltpu.SemaphoreType.DMA],
        compiler_params=params(42),
        cost_estimate=pl.CostEstimate(flops=10**9, bytes_accessed=12 * 2**20, transcendentals=0),
    )(x, weight, after)
    return made[:4] + made[8:], made[4:8]


def call_strips(far, near, padded):
    scratch = [pltpu.VMEM((WIDTH, 128), BF)] * 2
    scratch += [pltpu.VMEM((g.channels, g.sides), BF) for g in GEO]
    scratch += [pltpu.VMEM((g.channels, g.padded), BF) for g in GEO]
    scratch += [pltpu.VMEM((g.channels, g.slot), BF) for g in GEO]
    return pl.pallas_call(
        strips_kernel,
        out_shape=like((4, SLOT_ROWS, 128))[0],
        in_specs=[VMEM] * (2 + len(padded)),
        out_specs=VMEM,
        scratch_shapes=scratch,
        compiler_params=params(),
    )(far, near, *padded)


def call_block(strips, bias, weights):
    scratch = [pltpu.VMEM((3 * g.channels, g.lanes), BF) for g in GEO]
    scratch += [pltpu.VMEM((3 * g.channels, g.n1), BF) for g in GEO]
    scratch += [pltpu.VMEM((WIDTH, GEO[0].n2), BF)]
    scratch += [pltpu.VMEM((g.n2, g.channels), F32) for g in GEO[1:]]
    return pl.pallas_call(
        block_kernel,
        out_shape=like((4, 384, 128))[0],
        in_specs=[VMEM] * 6,
        out_specs=VMEM,
        scratch_shapes=scratch,
        compiler_params=params(),
    )(strips, bias, *weights)


def call_join(received, weight, bias):
    return pl.pallas_call(
        join_kernel,
        out_shape=like((WIDTH, 8, 128), (256, 96), (64, 192), (16, 384)),
        in_specs=[VMEM] * 3,
        out_specs=(VMEM,) * 4,
        scratch_shapes=[
            pltpu.VMEM((WIDTH, 1024), BF),
            pltpu.VMEM((WIDTH, 8, 128), F32),
        ],
        compiler_params=params(),
    )(received, weight, bias)


def paired(shard, first):
    size = lax.axis_size("col")
    pairs = []
    for c in range(first, size - 1, 2):
        pairs += [(c, c + 1), (c + 1, c)]
    return lax.ppermute(shard, "col", pairs)


def swapped(parts, axis):
    return lax.all_to_all(parts, axis, split_axis=0, concat_axis=0, tiled=True)


def local(section_in, conv_weight, conv_bias, join_weight, join_bias):
    x = section_in[0, 0, 0]
    far, near = call_cols(x)
    padded, weights = call_prepare(x, conv_weight, far)
    strips = call_strips(paired(far, 1), paired(near, 0), padded)
    settled = call_block(swapped(strips, "row"), conv_bias, weights)
    out = call_join(swapped(settled, "branch"), join_weight, join_bias[None, :])
    first = [out[0]]
    for g in GEO[1:]:
        pixel_major = out[g.b].reshape(g.strip, g.cols, g.channels)
        first.append(pixel_major.transpose(2, 0, 1))
    return tuple(first)


def solution(mesh):
    in_specs = (
        P("branch", "row", "col", None, None),
        P("branch", None, None, None, None, None),
        P("branch", None, None),
        P(),
        P(),
    )
    out_specs = (P(None, ("branch", "row"), "col"),) * 4
    return jax.shard_map(local, mesh=mesh, in_specs=in_specs, out_specs=out_specs, check_vma=False)
```

```python
import jax
import jax.numpy as jnp
from jax import lax
from jax.experimental import pallas as pl
from jax.experimental.pallas import tpu as pltpu
from jax.sharding import PartitionSpec as P

WIDTH = 48
TH = 32
TW = 128
BF = jnp.bfloat16
F32 = jnp.float32
VMEM = pl.BlockSpec(memory_space=pltpu.VMEM)


def up128(n):
    return -(-n // 128) * 128


class Geo:
    def __init__(self, b):
        self.b = b
        self.parts = 1 << b
        self.channels = WIDTH << b
        self.rows = TH >> b
        self.cols = TW >> b
        self.pixels = self.rows * self.cols
        self.strip = self.rows // 4
        self.high = self.strip + 4
        self.pitch = self.cols + 4
        self.padded = up128(self.rows * self.pitch)
        self.sides = 4 * self.rows
        self.slot = up128(self.high * self.pitch)
        self.blocks = self.slot // 128
        self.wide = up128(4 * self.pitch)
        self.lanes = self.high * self.wide
        self.n1 = (self.strip + 2) * self.wide
        self.n2 = self.strip * self.wide
        self.start = ((1 << b) - 1) * WIDTH


GEO = [Geo(b) for b in range(4)]
SLOT_ROWS = 624
PREPARE_MIB = 42
STEPS = (640, 768, 512, 384)


def place():
    return lax.axis_index("branch"), lax.axis_index("row"), lax.axis_index("col")


def per_branch(body):
    branch = place()[0]
    for g in GEO:

        @pl.when(branch == g.b)
        def _(g=g):
            body(g)


def cols_kernel(x, far, near, west, east):
    def body(g):
        for q in range(g.parts):
            for y in range(g.rows):
                lane = q * g.pixels + y * g.cols
                at = 2 * (q * g.rows + y)
                west[:, at : at + 2] = x[:, lane : lane + 2]
                last = lane + g.cols - 2
                east[:, at : at + 2] = x[:, last : last + 2]

    per_branch(body)
    odd = place()[2] % 2

    @pl.when(odd == 0)
    def _():
        far[...] = west[...]
        near[...] = east[...]

    @pl.when(odd == 1)
    def _():
        far[...] = east[...]
        near[...] = west[...]


def channel_order(g):
    out = lax.broadcasted_iota(jnp.int32, (g.channels, g.channels), 0)
    k = lax.broadcasted_iota(jnp.int32, (g.channels, g.channels), 1)
    part = jnp.zeros_like(k)
    for m in range(1, g.parts):
        part = part + (k >= WIDTH * m).astype(jnp.int32)
    at = (k - WIDTH * part) * g.parts + part
    return (at == out).astype(F32).astype(BF)


def side_places(g):
    n = lax.broadcasted_iota(jnp.int32, (1, g.padded), 1).astype(F32)
    y = jnp.floor((n + 0.5) * (1.0 / g.pitch))
    x = n - y * g.pitch
    right = x > g.cols + 1.0
    spot = 2.0 * y + jnp.where(right, x - (g.cols + 2.0) + 2.0 * g.rows, x)
    spot = jnp.where(((x < 2.0) | right) & (y < g.rows), spot, -1.0)
    k = lax.broadcasted_iota(jnp.int32, (g.sides, g.padded), 0).astype(F32)
    return (k == spot).astype(F32).astype(BF)


def prepare_kernel(x_hbm, weight, _, *refs):
    xp_all, wp_all, places, orders = refs[:4], refs[4:8], refs[8:12], (None,) + refs[12:15]
    wbuf, sems, x, x_sem = refs[18:]
    st_all = (x,) + refs[15:18]
    copy = pltpu.make_async_copy(x_hbm, x, x_sem)
    copy.start()

    def body(g):
        c = g.channels
        st, xp, wp = st_all[g.b], xp_all[g.b], wp_all[g.b]
        cl = up128(c)

        def fetch(layer):
            return pltpu.make_async_copy(
                weight.at[0, layer, :, :, 0:c, 0:cl],
                wbuf.at[layer, :, :, 0:c, 0:cl],
                sems.at[layer],
            )

        def fetch_tap(n):
            layer, dy, dx = n // 9, n // 3 % 3, n % 3
            return pltpu.make_async_copy(
                weight.at[0, layer, dy, dx],
                wp.at[layer, dy, :, c * dx : c * (dx + 1)],
                sems.at[n],
            )

        fetches = [fetch_tap(n) for n in range(18)] if g.b == 3 else [fetch(0), fetch(1)]
        for each in fetches:
            each.start()
        places[g.b][...] = side_places(g)
        if g.b:
            order = channel_order(g)
            orders[g.b][...] = order
        xp[...] = jnp.zeros_like(xp)
        copy.wait()
        if g.b:
            for q in range(g.parts):
                st[q * WIDTH : (q + 1) * WIDTH, :] = x[:, q * g.pixels : (q + 1) * g.pixels]
            st[...] = nn(order, st[...]).astype(BF)
        for y in range(g.rows):
            to = y * g.pitch + 2
            xp[:, to : to + g.cols] = st[:, y * g.cols : (y + 1) * g.cols]
        for each in fetches:
            each.wait()
        for layer in range(2 if g.b < 3 else 0):
            for dy in range(3):
                for dx in range(3):
                    tap = wbuf[layer, dy, dx, 0:c, 0:c]
                    wp[layer, dy, :, c * dx : c * (dx + 1)] = tap

    per_branch(body)


def runs(g, k):
    i = 0
    while i < g.high:
        y = (k * g.strip - 2 + i) % g.rows
        n = min(g.high - i, g.rows - y)
        yield i, y, n
        i += n


def strips_kernel(far, near, *refs):
    xp_all, places, orders, out = refs[:4], refs[4:8], (None,) + refs[8:11], refs[11]
    left, right = refs[12:14]
    st_all, xf_all, slot_all = refs[14:18], refs[18:22], refs[22:26]
    odd = place()[2] % 2

    @pl.when(odd == 0)
    def _():
        left[...] = far[...]
        right[...] = near[...]

    @pl.when(odd == 1)
    def _():
        left[...] = near[...]
        right[...] = far[...]

    def body(g):
        c, n = g.channels, 2 * g.rows
        st, xf, slot = st_all[g.b], xf_all[g.b], slot_all[g.b]
        for q in range(g.parts):
            for s, ref in enumerate((left, right)):
                st[q * WIDTH : (q + 1) * WIDTH, s * n : (s + 1) * n] = ref[:, q * n : (q + 1) * n]
        stacked = st[...]
        if g.b:
            stacked = nn(orders[g.b][...], stacked).astype(BF)
        xf[...] = xp_all[g.b][...] + nn(stacked, places[g.b][...]).astype(BF)
        for k in range(4):
            for i, y, rows in runs(g, k):
                at, lane, size = i * g.pitch, y * g.pitch, rows * g.pitch
                slot[:, at : at + size] = xf[:, lane : lane + size]
            for m in range(g.blocks):
                out[k, m * c : (m + 1) * c, :] = slot[:, 128 * m : 128 * (m + 1)]

    per_branch(body)


def inside(g, row_place, col_place):
    p = lax.broadcasted_iota(jnp.int32, (8, g.n1), 1).astype(F32)
    row = jnp.floor((p + 0.5) * (1.0 / g.wide))
    rest = p - row * g.wide
    tile = jnp.floor((rest + 0.5) * (1.0 / g.pitch))
    x = rest - tile * g.pitch
    y = row - 1.0 + (row_place * g.strip).astype(F32)
    out = (
        ((tile == 0.0) & (y < 0.0))
        | ((tile == 3.0) & (y > g.rows - 1.0))
        | ((x == 1.0) & (col_place == 0))
        | ((x == g.cols + 2.0) & (col_place == 15))
    )
    return jnp.where(out, 0.0, 1.0)[0:1, :]


def block_kernel(strips, bias, *refs):
    wp_all, out = refs[:4], refs[4]
    xr_all, hr_all, z0, zt_all = refs[5:9], refs[9:13], refs[13], (None,) + refs[14:17]
    _, row_place, col_place = place()

    def body(g):
        c = g.channels
        cl = up128(c)
        xr, hr, wp = xr_all[g.b], hr_all[g.b], wp_all[g.b]

        def put(i, tile, source):
            lane, to, left = i * g.pitch, i * g.wide + tile * g.pitch, g.pitch
            while left:
                m, at = divmod(lane, 128)
                n = min(left, 128 - at)
                if 0 <= source < 4:
                    piece = strips[source, m * c : (m + 1) * c, at : at + n]
                else:
                    piece = jnp.zeros((c, n), BF)
                xr[c : 2 * c, to : to + n] = piece
                lane, to, left = lane + n, to + n, left - n

        for i in range(g.high):
            low = [k for k in range(4) if k * g.strip - 2 + i < 0]
            high = [k for k in range(4) if k * g.strip - 2 + i >= g.rows]
            for tile in range(4):
                put(i, tile, tile)
            if low:

                @pl.when(row_place <= max(low))
                def _(i=i):
                    for tile in range(4):
                        put(i, tile, tile - 1)

            if high:

                @pl.when(row_place >= min(high))
                def _(i=i):
                    for tile in range(4):
                        put(i, tile, tile + 1)

        mask = inside(g, row_place, col_place)

        def column(layer):
            wide = jnp.broadcast_to(bias[0, layer : layer + 1, :], (8, 8 * WIDTH))
            return wide.T[0:c, 0:1]

        def conv(layer, maps, size, n, finish):
            maps[0:c, 1:size] = maps[c : 2 * c, 0 : size - 1]
            maps[2 * c : 3 * c, 0 : size - 1] = maps[c : 2 * c, 1:size]
            thirds = [slice(0, 3 * c)]
            if g.b == 3:
                thirds = [slice(c * third, c * (third + 1)) for third in (1, 0, 2)]
            step = STEPS[g.b]
            for at in range(0, n, step):
                width = min(step, n - at)
                total = None
                for part in thirds:
                    for dy in range(3):
                        lane = at + dy * g.wide
                        term = nn(wp[layer, dy, :, part], maps[part, lane : lane + width])
                        total = term if total is None else total + term
                finish(at, width, total)

        bias0 = column(0)

        def finish_first(at, size, total):
            h = jnp.maximum(total + bias0, 0.0) * mask[:, at : at + size]
            hr[c : 2 * c, at : at + size] = h.astype(BF)

        conv(0, xr, g.lanes, g.n1, finish_first)

        bias1 = column(1)

        def finish_second(at, size, total):
            lane = 2 * g.wide + at
            z = jnp.maximum(total + bias1 + xr[c : 2 * c, lane : lane + size].astype(F32), 0.0)
            if g.b == 0:
                z0[:, at : at + size] = z.astype(BF)
            else:
                zt_all[g.b][at : at + size, :] = z.T

        conv(1, hr, g.n1, g.n2, finish_second)

        for tile in range(4):
            for i in range(g.strip):
                at = i * g.wide + tile * g.pitch + 2
                if g.b == 0:
                    out[tile, i * WIDTH : (i + 1) * WIDTH, :] = z0[:, at : at + g.cols]
                    continue
                values = zt_all[g.b][at : at + g.cols, :].astype(BF)
                for m in range(cl // 128):
                    r = (m * g.strip + i) * g.cols
                    lanes = min(128, c - 128 * m)
                    out[tile, r : r + g.cols, 0:lanes] = values[:, 128 * m : 128 * m + lanes]

    per_branch(body)


def repeat_map(j, i):
    gj, gi = GEO[j], GEO[i]
    shape = (gj.pixels // 4, gi.pixels // 4)
    fine = lax.broadcasted_iota(jnp.int32, shape, 0)
    coarse = lax.broadcasted_iota(jnp.int32, shape, 1)
    return cover(fine, coarse, gj, i - j)


def cover(fine, coarse, g, d):
    bits = 7 - g.b
    y = fine >> bits
    x = fine & (g.cols - 1)
    return (((y >> d) << (bits - d)) + (x >> d) == coarse).astype(F32).astype(BF)


def repeat_map_t(j, i):
    gj, gi = GEO[j], GEO[i]
    shape = (gi.pixels // 4, gj.pixels // 4)
    coarse = lax.broadcasted_iota(jnp.int32, shape, 0)
    fine = lax.broadcasted_iota(jnp.int32, shape, 1)
    return cover(fine, coarse, gj, i - j)


def nn(a, b):
    return jnp.dot(a, b, preferred_element_type=F32)


def nt(a, b):
    return lax.dot_general(a, b, (((1,), (1,)), ((), ())), preferred_element_type=F32)


def join_kernel(zb, weight, bias, out0, out1, out2, out3, z0s, s0):
    for y in range(8):
        z0s[:, 128 * y : 128 * (y + 1)] = zb[0, WIDTH * y : WIDTH * (y + 1), :]
    z = [
        z0s[...],
        zb[1, 0:256, 0:96],
        jnp.concatenate([zb[2, 0:64, :], zb[2, 64:128, 0:64]], axis=1),
        jnp.concatenate([zb[3, 0:16, :], zb[3, 16:32, :], zb[3, 32:48, :]], axis=1),
    ]

    def block(j, i, last=None):
        first, end = GEO[j], GEO[j if last is None else last]
        gi = GEO[i]
        rows = slice(first.start, end.start + end.channels)
        return weight[rows, gi.start : gi.start + gi.channels]

    def tn(a, b):
        return lax.dot_general(a, b, (((0,), (0,)), ((), ())), preferred_element_type=F32)

    size = [g.pixels // 4 for g in GEO]
    terms = {i: nt(z[i], block(0, i, i - 1)).astype(BF) for i in (1, 2, 3)}
    shrink0 = jnp.concatenate([repeat_map_t(0, i) for i in (1, 2, 3)], axis=0)
    shrink1 = jnp.concatenate([repeat_map_t(1, i) for i in (2, 3)], axis=0)
    sums = {0: nt(shrink0, z[0]), 1: nn(shrink1, z[1]), 2: nn(repeat_map_t(2, 3), z[2])}

    stacked = jnp.concatenate([terms[i][:, 0:WIDTH] for i in (1, 2, 3)], axis=0)
    wide = jnp.broadcast_to(bias[:, 0:WIDTH], (8, WIDTH))
    total = tn(stacked, shrink0) + z[0].astype(F32) + wide.T[:, 0:1]
    total = jnp.maximum(total, 0.0)
    for y in range(8):
        s0[:, y, :] = total[:, 128 * y : 128 * (y + 1)]
    out0[...] = s0[...].astype(BF)

    for j, out in ((1, out1), (2, out2), (3, out3)):
        g = GEO[j]
        total = z[j].astype(F32) + bias[:, g.start : g.start + g.channels]
        for i in range(j):
            first = sum(size[i + 1 : j])
            mean = (sums[i][first : first + size[j], :] * (0.25 ** (j - i))).astype(BF)
            total = total + nt(mean, block(j, i)).astype(BF).astype(F32)
        for i in range(j + 1, 4):
            term = terms[i][:, g.start : g.start + g.channels]
            total = total + nn(repeat_map(j, i), term)
        out[...] = jnp.maximum(total, 0.0).astype(BF)


def params(mib=24):
    return pltpu.CompilerParams(vmem_limit_bytes=mib * 1024 * 1024)


def like(*shapes):
    return tuple(jax.ShapeDtypeStruct(s, BF) for s in shapes)


def call_cols(x):
    return pl.pallas_call(
        cols_kernel,
        out_shape=like((WIDTH, 128), (WIDTH, 128)),
        in_specs=[VMEM],
        out_specs=(VMEM, VMEM),
        scratch_shapes=[pltpu.VMEM((WIDTH, 128), BF)] * 2,
        compiler_params=params(),
    )(x)


def call_prepare(x, weight, after):
    shapes = [(g.channels, g.padded) for g in GEO]
    shapes += [(2, 3, g.channels, 3 * g.channels) for g in GEO]
    shapes += [(g.sides, g.padded) for g in GEO]
    shapes += [(g.channels, g.channels) for g in GEO[1:]]
    made = pl.pallas_call(
        prepare_kernel,
        out_shape=like(*shapes),
        in_specs=[pl.BlockSpec(memory_space=pltpu.HBM)] * 2 + [pl.BlockSpec(memory_space=pl.ANY)],
        out_specs=(VMEM,) * len(shapes),
        scratch_shapes=[pltpu.VMEM((g.channels, g.pixels), BF) for g in GEO[1:]]
        + [pltpu.VMEM((2, 3, 3, 192, 256), BF), pltpu.SemaphoreType.DMA((18,))]
        + [pltpu.VMEM((WIDTH, TH * TW), BF), pltpu.SemaphoreType.DMA],
        compiler_params=params(PREPARE_MIB),
        cost_estimate=pl.CostEstimate(flops=10**9, bytes_accessed=12 * 2**20, transcendentals=0),
    )(x, weight, after)
    return made[:4] + made[8:], made[4:8]


def call_strips(far, near, padded):
    scratch = [pltpu.VMEM((WIDTH, 128), BF)] * 2
    scratch += [pltpu.VMEM((g.channels, g.sides), BF) for g in GEO]
    scratch += [pltpu.VMEM((g.channels, g.padded), BF) for g in GEO]
    scratch += [pltpu.VMEM((g.channels, g.slot), BF) for g in GEO]
    return pl.pallas_call(
        strips_kernel,
        out_shape=like((4, SLOT_ROWS, 128))[0],
        in_specs=[VMEM] * (2 + len(padded)),
        out_specs=VMEM,
        scratch_shapes=scratch,
        compiler_params=params(),
    )(far, near, *padded)


def call_block(strips, bias, weights):
    scratch = [pltpu.VMEM((3 * g.channels, g.lanes), BF) for g in GEO]
    scratch += [pltpu.VMEM((3 * g.channels, g.n1), BF) for g in GEO]
    scratch += [pltpu.VMEM((WIDTH, GEO[0].n2), BF)]
    scratch += [pltpu.VMEM((g.n2, g.channels), F32) for g in GEO[1:]]
    return pl.pallas_call(
        block_kernel,
        out_shape=like((4, 384, 128))[0],
        in_specs=[VMEM] * 6,
        out_specs=VMEM,
        scratch_shapes=scratch,
        compiler_params=params(),
    )(strips, bias, *weights)


def call_join(received, weight, bias):
    return pl.pallas_call(
        join_kernel,
        out_shape=like((WIDTH, 8, 128), (256, 96), (64, 192), (16, 384)),
        in_specs=[VMEM] * 3,
        out_specs=(VMEM,) * 4,
        scratch_shapes=[
            pltpu.VMEM((WIDTH, 1024), BF),
            pltpu.VMEM((WIDTH, 8, 128), F32),
        ],
        compiler_params=params(),
    )(received, weight, bias)


def paired(shard, first):
    size = lax.axis_size("col")
    pairs = []
    for c in range(first, size - 1, 2):
        pairs += [(c, c + 1), (c + 1, c)]
    return lax.ppermute(shard, "col", pairs)


def swapped(parts, axis):
    return lax.all_to_all(parts, axis, split_axis=0, concat_axis=0, tiled=True)


def local(section_in, conv_weight, conv_bias, join_weight, join_bias):
    x = section_in[0, 0, 0]
    far, near = call_cols(x)
    padded, weights = call_prepare(x, conv_weight, far)
    strips = call_strips(paired(far, 1), paired(near, 0), padded)
    settled = call_block(swapped(strips, "row"), conv_bias, weights)
    out = call_join(swapped(settled, "branch"), join_weight, join_bias[None, :])
    first = [out[0]]
    for g in GEO[1:]:
        pixel_major = out[g.b].reshape(g.strip, g.cols, g.channels)
        first.append(pixel_major.transpose(2, 0, 1))
    return tuple(first)


def solution(mesh):
    in_specs = (
        P("branch", "row", "col", None, None),
        P("branch", None, None, None, None, None),
        P("branch", None, None),
        P(),
        P(),
    )
    out_specs = (P(None, ("branch", "row"), "col"),) * 4
    return jax.shard_map(local, mesh=mesh, in_specs=in_specs, out_specs=out_specs, check_vma=False)
```

```python
import jax
import jax.numpy as jnp
from jax import lax
from jax.experimental import pallas as pl
from jax.experimental.pallas import tpu as pltpu
from jax.sharding import PartitionSpec as P

WIDTH = 48
TH = 32
TW = 128
BF = jnp.bfloat16
F32 = jnp.float32
VMEM = pl.BlockSpec(memory_space=pltpu.VMEM)


def up128(n):
    return -(-n // 128) * 128


class Geo:
    def __init__(self, b):
        self.b = b
        self.parts = 1 << b
        self.channels = WIDTH << b
        self.rows = TH >> b
        self.cols = TW >> b
        self.pixels = self.rows * self.cols
        self.strip = self.rows // 4
        self.high = self.strip + 4
        self.pitch = self.cols + 4
        self.padded = up128(self.rows * self.pitch)
        self.sides = 4 * self.rows
        self.slot = up128(self.high * self.pitch)
        self.blocks = self.slot // 128
        self.wide = up128(4 * self.pitch)
        self.lanes = self.high * self.wide
        self.n1 = (self.strip + 2) * self.wide
        self.n2 = self.strip * self.wide
        self.start = ((1 << b) - 1) * WIDTH


GEO = [Geo(b) for b in range(4)]
SLOT_ROWS = 624
PREPARE_MIB = 42
STEPS = (640, 768, 512, 384)


def place():
    return lax.axis_index("branch"), lax.axis_index("row"), lax.axis_index("col")


def per_branch(body):
    branch = place()[0]
    for g in GEO:

        @pl.when(branch == g.b)
        def _(g=g):
            body(g)


def cols_kernel(x, far, near, kept, west, east):
    def body(g):
        for q in range(g.parts):
            for y in range(g.rows):
                lane = q * g.pixels + y * g.cols
                at = 2 * (q * g.rows + y)
                west[:, at : at + 2] = x[:, lane : lane + 2]
                last = lane + g.cols - 2
                east[:, at : at + 2] = x[:, last : last + 2]

    per_branch(body)
    kept[...] = x[...]
    odd = place()[2] % 2

    @pl.when(odd == 0)
    def _():
        far[...] = west[...]
        near[...] = east[...]

    @pl.when(odd == 1)
    def _():
        far[...] = east[...]
        near[...] = west[...]


def channel_order(g):
    out = lax.broadcasted_iota(jnp.int32, (g.channels, g.channels), 0)
    k = lax.broadcasted_iota(jnp.int32, (g.channels, g.channels), 1)
    part = jnp.zeros_like(k)
    for m in range(1, g.parts):
        part = part + (k >= WIDTH * m).astype(jnp.int32)
    at = (k - WIDTH * part) * g.parts + part
    return (at == out).astype(F32).astype(BF)


def side_places(g):
    n = lax.broadcasted_iota(jnp.int32, (1, g.padded), 1).astype(F32)
    y = jnp.floor((n + 0.5) * (1.0 / g.pitch))
    x = n - y * g.pitch
    right = x > g.cols + 1.0
    spot = 2.0 * y + jnp.where(right, x - (g.cols + 2.0) + 2.0 * g.rows, x)
    spot = jnp.where(((x < 2.0) | right) & (y < g.rows), spot, -1.0)
    k = lax.broadcasted_iota(jnp.int32, (g.sides, g.padded), 0).astype(F32)
    return (k == spot).astype(F32).astype(BF)


def prepare_kernel(x, weight, *refs):
    xp_all, wp_all, places, orders = refs[:4], refs[4:8], refs[8:12], (None,) + refs[12:15]
    st_all, wbuf, sems = (x,) + refs[15:18], refs[18], refs[19]

    def body(g):
        c = g.channels
        st, xp, wp = st_all[g.b], xp_all[g.b], wp_all[g.b]
        cl = up128(c)

        def fetch(layer):
            return pltpu.make_async_copy(
                weight.at[0, layer, :, :, 0:c, 0:cl],
                wbuf.at[layer, :, :, 0:c, 0:cl],
                sems.at[layer],
            )

        def fetch_tap(n):
            layer, dy, dx = n // 9, n // 3 % 3, n % 3
            return pltpu.make_async_copy(
                weight.at[0, layer, dy, dx],
                wp.at[layer, dy, :, c * dx : c * (dx + 1)],
                sems.at[n],
            )

        fetches = [fetch_tap(n) for n in range(18)] if g.b == 3 else [fetch(0), fetch(1)]
        for each in fetches:
            each.start()
        places[g.b][...] = side_places(g)
        if g.b:
            order = channel_order(g)
            orders[g.b][...] = order
        xp[...] = jnp.zeros_like(xp)
        if g.b:
            for q in range(g.parts):
                st[q * WIDTH : (q + 1) * WIDTH, :] = x[:, q * g.pixels : (q + 1) * g.pixels]
            st[...] = nn(order, st[...]).astype(BF)
        for y in range(g.rows):
            to = y * g.pitch + 2
            xp[:, to : to + g.cols] = st[:, y * g.cols : (y + 1) * g.cols]
        for each in fetches:
            each.wait()
        for layer in range(2 if g.b < 3 else 0):
            for dy in range(3):
                for dx in range(3):
                    tap = wbuf[layer, dy, dx, 0:c, 0:c]
                    wp[layer, dy, :, c * dx : c * (dx + 1)] = tap

    per_branch(body)


def runs(g, k):
    i = 0
    while i < g.high:
        y = (k * g.strip - 2 + i) % g.rows
        n = min(g.high - i, g.rows - y)
        yield i, y, n
        i += n


def strips_kernel(far, near, *refs):
    xp_all, places, orders, out = refs[:4], refs[4:8], (None,) + refs[8:11], refs[11]
    left, right = refs[12:14]
    st_all, xf_all, slot_all = refs[14:18], refs[18:22], refs[22:26]
    odd = place()[2] % 2

    @pl.when(odd == 0)
    def _():
        left[...] = far[...]
        right[...] = near[...]

    @pl.when(odd == 1)
    def _():
        left[...] = near[...]
        right[...] = far[...]

    def body(g):
        c, n = g.channels, 2 * g.rows
        st, xf, slot = st_all[g.b], xf_all[g.b], slot_all[g.b]
        for q in range(g.parts):
            for s, ref in enumerate((left, right)):
                st[q * WIDTH : (q + 1) * WIDTH, s * n : (s + 1) * n] = ref[:, q * n : (q + 1) * n]
        stacked = st[...]
        if g.b:
            stacked = nn(orders[g.b][...], stacked).astype(BF)
        xf[...] = xp_all[g.b][...] + nn(stacked, places[g.b][...]).astype(BF)
        for k in range(4):
            for i, y, rows in runs(g, k):
                at, lane, size = i * g.pitch, y * g.pitch, rows * g.pitch
                slot[:, at : at + size] = xf[:, lane : lane + size]
            for m in range(g.blocks):
                out[k, m * c : (m + 1) * c, :] = slot[:, 128 * m : 128 * (m + 1)]

    per_branch(body)


def inside(g, row_place, col_place):
    p = lax.broadcasted_iota(jnp.int32, (8, g.n1), 1).astype(F32)
    row = jnp.floor((p + 0.5) * (1.0 / g.wide))
    rest = p - row * g.wide
    tile = jnp.floor((rest + 0.5) * (1.0 / g.pitch))
    x = rest - tile * g.pitch
    y = row - 1.0 + (row_place * g.strip).astype(F32)
    out = (
        ((tile == 0.0) & (y < 0.0))
        | ((tile == 3.0) & (y > g.rows - 1.0))
        | ((x == 1.0) & (col_place == 0))
        | ((x == g.cols + 2.0) & (col_place == 15))
    )
    return jnp.where(out, 0.0, 1.0)[0:1, :]


def block_kernel(strips, bias, *refs):
    wp_all, out = refs[:4], refs[4]
    xr_all, hr_all, z0, zt_all = refs[5:9], refs[9:13], refs[13], (None,) + refs[14:17]
    _, row_place, col_place = place()

    def body(g):
        c = g.channels
        cl = up128(c)
        xr, hr, wp = xr_all[g.b], hr_all[g.b], wp_all[g.b]

        def put(i, tile, source):
            lane, to, left = i * g.pitch, i * g.wide + tile * g.pitch, g.pitch
            while left:
                m, at = divmod(lane, 128)
                n = min(left, 128 - at)
                if 0 <= source < 4:
                    piece = strips[source, m * c : (m + 1) * c, at : at + n]
                else:
                    piece = jnp.zeros((c, n), BF)
                xr[c : 2 * c, to : to + n] = piece
                lane, to, left = lane + n, to + n, left - n

        for i in range(g.high):
            low = [k for k in range(4) if k * g.strip - 2 + i < 0]
            high = [k for k in range(4) if k * g.strip - 2 + i >= g.rows]
            for tile in range(4):
                put(i, tile, tile)
            if low:

                @pl.when(row_place <= max(low))
                def _(i=i):
                    for tile in range(4):
                        put(i, tile, tile - 1)

            if high:

                @pl.when(row_place >= min(high))
                def _(i=i):
                    for tile in range(4):
                        put(i, tile, tile + 1)

        mask = inside(g, row_place, col_place)

        def column(layer):
            wide = jnp.broadcast_to(bias[0, layer : layer + 1, :], (8, 8 * WIDTH))
            return wide.T[0:c, 0:1]

        def conv(layer, maps, size, n, finish):
            maps[0:c, 1:size] = maps[c : 2 * c, 0 : size - 1]
            maps[2 * c : 3 * c, 0 : size - 1] = maps[c : 2 * c, 1:size]
            thirds = [slice(0, 3 * c)]
            if g.b == 3:
                thirds = [slice(c * third, c * (third + 1)) for third in (1, 0, 2)]
            step = STEPS[g.b]
            for at in range(0, n, step):
                width = min(step, n - at)
                total = None
                for part in thirds:
                    for dy in range(3):
                        lane = at + dy * g.wide
                        term = nn(wp[layer, dy, :, part], maps[part, lane : lane + width])
                        total = term if total is None else total + term
                finish(at, width, total)

        bias0 = column(0)

        def finish_first(at, size, total):
            h = jnp.maximum(total + bias0, 0.0) * mask[:, at : at + size]
            hr[c : 2 * c, at : at + size] = h.astype(BF)

        conv(0, xr, g.lanes, g.n1, finish_first)

        bias1 = column(1)

        def finish_second(at, size, total):
            lane = 2 * g.wide + at
            z = jnp.maximum(total + bias1 + xr[c : 2 * c, lane : lane + size].astype(F32), 0.0)
            if g.b == 0:
                z0[:, at : at + size] = z.astype(BF)
            else:
                zt_all[g.b][at : at + size, :] = z.T

        conv(1, hr, g.n1, g.n2, finish_second)

        for tile in range(4):
            for i in range(g.strip):
                at = i * g.wide + tile * g.pitch + 2
                if g.b == 0:
                    out[tile, i * WIDTH : (i + 1) * WIDTH, :] = z0[:, at : at + g.cols]
                    continue
                values = zt_all[g.b][at : at + g.cols, :].astype(BF)
                for m in range(cl // 128):
                    r = (m * g.strip + i) * g.cols
                    lanes = min(128, c - 128 * m)
                    out[tile, r : r + g.cols, 0:lanes] = values[:, 128 * m : 128 * m + lanes]

    per_branch(body)


def repeat_map(j, i):
    gj, gi = GEO[j], GEO[i]
    shape = (gj.pixels // 4, gi.pixels // 4)
    fine = lax.broadcasted_iota(jnp.int32, shape, 0)
    coarse = lax.broadcasted_iota(jnp.int32, shape, 1)
    return cover(fine, coarse, gj, i - j)


def cover(fine, coarse, g, d):
    bits = 7 - g.b
    y = fine >> bits
    x = fine & (g.cols - 1)
    return (((y >> d) << (bits - d)) + (x >> d) == coarse).astype(F32).astype(BF)


def repeat_map_t(j, i):
    gj, gi = GEO[j], GEO[i]
    shape = (gi.pixels // 4, gj.pixels // 4)
    coarse = lax.broadcasted_iota(jnp.int32, shape, 0)
    fine = lax.broadcasted_iota(jnp.int32, shape, 1)
    return cover(fine, coarse, gj, i - j)


def nn(a, b):
    return jnp.dot(a, b, preferred_element_type=F32)


def nt(a, b):
    return lax.dot_general(a, b, (((1,), (1,)), ((), ())), preferred_element_type=F32)


def join_kernel(zb, weight, bias, out0, out1, out2, out3, z0s, s0):
    for y in range(8):
        z0s[:, 128 * y : 128 * (y + 1)] = zb[0, WIDTH * y : WIDTH * (y + 1), :]
    z = [
        z0s[...],
        zb[1, 0:256, 0:96],
        jnp.concatenate([zb[2, 0:64, :], zb[2, 64:128, 0:64]], axis=1),
        jnp.concatenate([zb[3, 0:16, :], zb[3, 16:32, :], zb[3, 32:48, :]], axis=1),
    ]

    def block(j, i, last=None):
        first, end = GEO[j], GEO[j if last is None else last]
        gi = GEO[i]
        rows = slice(first.start, end.start + end.channels)
        return weight[rows, gi.start : gi.start + gi.channels]

    def tn(a, b):
        return lax.dot_general(a, b, (((0,), (0,)), ((), ())), preferred_element_type=F32)

    size = [g.pixels // 4 for g in GEO]
    terms = {i: nt(z[i], block(0, i, i - 1)).astype(BF) for i in (1, 2, 3)}
    shrink0 = jnp.concatenate([repeat_map_t(0, i) for i in (1, 2, 3)], axis=0)
    shrink1 = jnp.concatenate([repeat_map_t(1, i) for i in (2, 3)], axis=0)
    sums = {0: nt(shrink0, z[0]), 1: nn(shrink1, z[1]), 2: nn(repeat_map_t(2, 3), z[2])}

    stacked = jnp.concatenate([terms[i][:, 0:WIDTH] for i in (1, 2, 3)], axis=0)
    wide = jnp.broadcast_to(bias[:, 0:WIDTH], (8, WIDTH))
    total = tn(stacked, shrink0) + z[0].astype(F32) + wide.T[:, 0:1]
    total = jnp.maximum(total, 0.0)
    for y in range(8):
        s0[:, y, :] = total[:, 128 * y : 128 * (y + 1)]
    out0[...] = s0[...].astype(BF)

    for j, out in ((1, out1), (2, out2), (3, out3)):
        g = GEO[j]
        total = z[j].astype(F32) + bias[:, g.start : g.start + g.channels]
        for i in range(j):
            first = sum(size[i + 1 : j])
            mean = (sums[i][first : first + size[j], :] * (0.25 ** (j - i))).astype(BF)
            total = total + nt(mean, block(j, i)).astype(BF).astype(F32)
        for i in range(j + 1, 4):
            term = terms[i][:, g.start : g.start + g.channels]
            total = total + nn(repeat_map(j, i), term)
        out[...] = jnp.maximum(total, 0.0).astype(BF)


def params(mib=24):
    return pltpu.CompilerParams(vmem_limit_bytes=mib * 1024 * 1024)


def like(*shapes):
    return tuple(jax.ShapeDtypeStruct(s, BF) for s in shapes)


def call_cols(x):
    return pl.pallas_call(
        cols_kernel,
        out_shape=like((WIDTH, 128), (WIDTH, 128), (WIDTH, TH * TW)),
        in_specs=[VMEM],
        out_specs=(VMEM,) * 3,
        scratch_shapes=[pltpu.VMEM((WIDTH, 128), BF)] * 2,
        compiler_params=params(),
    )(x)


def call_prepare(x, weight):
    shapes = [(g.channels, g.padded) for g in GEO]
    shapes += [(2, 3, g.channels, 3 * g.channels) for g in GEO]
    shapes += [(g.sides, g.padded) for g in GEO]
    shapes += [(g.channels, g.channels) for g in GEO[1:]]
    made = pl.pallas_call(
        prepare_kernel,
        out_shape=like(*shapes),
        in_specs=[VMEM, pl.BlockSpec(memory_space=pltpu.HBM)],
        out_specs=(VMEM,) * len(shapes),
        scratch_shapes=[pltpu.VMEM((g.channels, g.pixels), BF) for g in GEO[1:]]
        + [pltpu.VMEM((2, 3, 3, 192, 256), BF), pltpu.SemaphoreType.DMA((18,))],
        compiler_params=params(PREPARE_MIB),
        cost_estimate=pl.CostEstimate(flops=10**9, bytes_accessed=12 * 2**20, transcendentals=0),
    )(x, weight)
    return made[:4] + made[8:], made[4:8]


def call_strips(far, near, padded):
    scratch = [pltpu.VMEM((WIDTH, 128), BF)] * 2
    scratch += [pltpu.VMEM((g.channels, g.sides), BF) for g in GEO]
    scratch += [pltpu.VMEM((g.channels, g.padded), BF) for g in GEO]
    scratch += [pltpu.VMEM((g.channels, g.slot), BF) for g in GEO]
    return pl.pallas_call(
        strips_kernel,
        out_shape=like((4, SLOT_ROWS, 128))[0],
        in_specs=[VMEM] * (2 + len(padded)),
        out_specs=VMEM,
        scratch_shapes=scratch,
        compiler_params=params(),
    )(far, near, *padded)


def call_block(strips, bias, weights):
    scratch = [pltpu.VMEM((3 * g.channels, g.lanes), BF) for g in GEO]
    scratch += [pltpu.VMEM((3 * g.channels, g.n1), BF) for g in GEO]
    scratch += [pltpu.VMEM((WIDTH, GEO[0].n2), BF)]
    scratch += [pltpu.VMEM((g.n2, g.channels), F32) for g in GEO[1:]]
    return pl.pallas_call(
        block_kernel,
        out_shape=like((4, 384, 128))[0],
        in_specs=[VMEM] * 6,
        out_specs=VMEM,
        scratch_shapes=scratch,
        compiler_params=params(),
    )(strips, bias, *weights)


def call_join(received, weight, bias):
    return pl.pallas_call(
        join_kernel,
        out_shape=like((WIDTH, 8, 128), (256, 96), (64, 192), (16, 384)),
        in_specs=[VMEM] * 3,
        out_specs=(VMEM,) * 4,
        scratch_shapes=[
            pltpu.VMEM((WIDTH, 1024), BF),
            pltpu.VMEM((WIDTH, 8, 128), F32),
        ],
        compiler_params=params(),
    )(received, weight, bias)


def paired(shard, first):
    size = lax.axis_size("col")
    pairs = []
    for c in range(first, size - 1, 2):
        pairs += [(c, c + 1), (c + 1, c)]
    return lax.ppermute(shard, "col", pairs)


def swapped(parts, axis):
    return lax.all_to_all(parts, axis, split_axis=0, concat_axis=0, tiled=True)


def local(section_in, conv_weight, conv_bias, join_weight, join_bias):
    x = section_in[0, 0, 0]
    far, near, kept = call_cols(x)
    padded, weights = call_prepare(kept, conv_weight)
    strips = call_strips(paired(far, 1), paired(near, 0), padded)
    settled = call_block(swapped(strips, "row"), conv_bias, weights)
    out = call_join(swapped(settled, "branch"), join_weight, join_bias[None, :])
    first = [out[0]]
    for g in GEO[1:]:
        pixel_major = out[g.b].reshape(g.strip, g.cols, g.channels)
        first.append(pixel_major.transpose(2, 0, 1))
    return tuple(first)


def solution(mesh):
    in_specs = (
        P("branch", "row", "col", None, None),
        P("branch", None, None, None, None, None),
        P("branch", None, None),
        P(),
        P(),
    )
    out_specs = (P(None, ("branch", "row"), "col"),) * 4
    return jax.shard_map(local, mesh=mesh, in_specs=in_specs, out_specs=out_specs, check_vma=False)
```

```python
import jax
import jax.numpy as jnp
from jax import lax
from jax.experimental import pallas as pl
from jax.experimental.pallas import tpu as pltpu
from jax.sharding import PartitionSpec as P

WIDTH = 48
TH = 32
TW = 128
BF = jnp.bfloat16
F32 = jnp.float32
VMEM = pl.BlockSpec(memory_space=pltpu.VMEM)


def up128(n):
    return -(-n // 128) * 128


class Geo:
    def __init__(self, b):
        self.b = b
        self.parts = 1 << b
        self.channels = WIDTH << b
        self.rows = TH >> b
        self.cols = TW >> b
        self.pixels = self.rows * self.cols
        self.strip = self.rows // 4
        self.high = self.strip + 4
        self.pitch = self.cols + 4
        self.padded = up128(self.rows * self.pitch)
        self.sides = 4 * self.rows
        self.slot = up128(self.high * self.pitch)
        self.blocks = self.slot // 128
        self.wide = up128(4 * self.pitch)
        self.lanes = self.high * self.wide
        self.n1 = (self.strip + 2) * self.wide
        self.n2 = self.strip * self.wide
        self.start = ((1 << b) - 1) * WIDTH


GEO = [Geo(b) for b in range(4)]
SLOT_ROWS = 624
PREPARE_MIB = 42
STEPS = (640, 768, 512, 256)


def place():
    return lax.axis_index("branch"), lax.axis_index("row"), lax.axis_index("col")


def per_branch(body):
    branch = place()[0]
    for g in GEO:

        @pl.when(branch == g.b)
        def _(g=g):
            body(g)


def cols_kernel(x, far, near, kept, west, east):
    def body(g):
        for q in range(g.parts):
            for y in range(g.rows):
                lane = q * g.pixels + y * g.cols
                at = 2 * (q * g.rows + y)
                west[:, at : at + 2] = x[:, lane : lane + 2]
                last = lane + g.cols - 2
                east[:, at : at + 2] = x[:, last : last + 2]

    per_branch(body)
    kept[...] = x[...]
    odd = place()[2] % 2

    @pl.when(odd == 0)
    def _():
        far[...] = west[...]
        near[...] = east[...]

    @pl.when(odd == 1)
    def _():
        far[...] = east[...]
        near[...] = west[...]


def channel_order(g):
    out = lax.broadcasted_iota(jnp.int32, (g.channels, g.channels), 0)
    k = lax.broadcasted_iota(jnp.int32, (g.channels, g.channels), 1)
    part = jnp.zeros_like(k)
    for m in range(1, g.parts):
        part = part + (k >= WIDTH * m).astype(jnp.int32)
    at = (k - WIDTH * part) * g.parts + part
    return (at == out).astype(F32).astype(BF)


def side_places(g):
    n = lax.broadcasted_iota(jnp.int32, (1, g.padded), 1).astype(F32)
    y = jnp.floor((n + 0.5) * (1.0 / g.pitch))
    x = n - y * g.pitch
    right = x > g.cols + 1.0
    spot = 2.0 * y + jnp.where(right, x - (g.cols + 2.0) + 2.0 * g.rows, x)
    spot = jnp.where(((x < 2.0) | right) & (y < g.rows), spot, -1.0)
    k = lax.broadcasted_iota(jnp.int32, (g.sides, g.padded), 0).astype(F32)
    return (k == spot).astype(F32).astype(BF)


def prepare_kernel(x, weight, *refs):
    xp_all, wp_all, places, orders = refs[:4], refs[4:8], refs[8:12], (None,) + refs[12:15]
    st_all, wbuf, sems = (x,) + refs[15:18], refs[18], refs[19]

    def body(g):
        c = g.channels
        st, xp, wp = st_all[g.b], xp_all[g.b], wp_all[g.b]
        cl = up128(c)

        def fetch(layer):
            return pltpu.make_async_copy(
                weight.at[0, layer, :, :, 0:c, 0:cl],
                wbuf.at[layer, :, :, 0:c, 0:cl],
                sems.at[layer],
            )

        def fetch_tap(n):
            layer, dy, dx = n // 9, n // 3 % 3, n % 3
            return pltpu.make_async_copy(
                weight.at[0, layer, dy, dx],
                wp.at[layer, dy, :, c * dx : c * (dx + 1)],
                sems.at[n],
            )

        fetches = [fetch_tap(n) for n in range(18)] if g.b == 3 else [fetch(0), fetch(1)]
        for each in fetches:
            each.start()
        places[g.b][...] = side_places(g)
        if g.b:
            order = channel_order(g)
            orders[g.b][...] = order
        xp[...] = jnp.zeros_like(xp)
        if g.b:
            for q in range(g.parts):
                st[q * WIDTH : (q + 1) * WIDTH, :] = x[:, q * g.pixels : (q + 1) * g.pixels]
            st[...] = nn(order, st[...]).astype(BF)
        for y in range(g.rows):
            to = y * g.pitch + 2
            xp[:, to : to + g.cols] = st[:, y * g.cols : (y + 1) * g.cols]
        for each in fetches:
            each.wait()
        for layer in range(2 if g.b < 3 else 0):
            for dy in range(3):
                for dx in range(3):
                    tap = wbuf[layer, dy, dx, 0:c, 0:c]
                    wp[layer, dy, :, c * dx : c * (dx + 1)] = tap

    per_branch(body)


def runs(g, k):
    i = 0
    while i < g.high:
        y = (k * g.strip - 2 + i) % g.rows
        n = min(g.high - i, g.rows - y)
        yield i, y, n
        i += n


def strips_kernel(far, near, *refs):
    xp_all, places, orders, out = refs[:4], refs[4:8], (None,) + refs[8:11], refs[11]
    left, right = refs[12:14]
    st_all, xf_all, slot_all = refs[14:18], refs[18:22], refs[22:26]
    odd = place()[2] % 2

    @pl.when(odd == 0)
    def _():
        left[...] = far[...]
        right[...] = near[...]

    @pl.when(odd == 1)
    def _():
        left[...] = near[...]
        right[...] = far[...]

    def body(g):
        c, n = g.channels, 2 * g.rows
        st, xf, slot = st_all[g.b], xf_all[g.b], slot_all[g.b]
        for q in range(g.parts):
            for s, ref in enumerate((left, right)):
                st[q * WIDTH : (q + 1) * WIDTH, s * n : (s + 1) * n] = ref[:, q * n : (q + 1) * n]
        stacked = st[...]
        if g.b:
            stacked = nn(orders[g.b][...], stacked).astype(BF)
        xf[...] = xp_all[g.b][...] + nn(stacked, places[g.b][...]).astype(BF)
        for k in range(4):
            for i, y, rows in runs(g, k):
                at, lane, size = i * g.pitch, y * g.pitch, rows * g.pitch
                slot[:, at : at + size] = xf[:, lane : lane + size]
            for m in range(g.blocks):
                out[k, m * c : (m + 1) * c, :] = slot[:, 128 * m : 128 * (m + 1)]

    per_branch(body)


def inside(g, row_place, col_place):
    p = lax.broadcasted_iota(jnp.int32, (8, g.n1), 1).astype(F32)
    row = jnp.floor((p + 0.5) * (1.0 / g.wide))
    rest = p - row * g.wide
    tile = jnp.floor((rest + 0.5) * (1.0 / g.pitch))
    x = rest - tile * g.pitch
    y = row - 1.0 + (row_place * g.strip).astype(F32)
    out = (
        ((tile == 0.0) & (y < 0.0))
        | ((tile == 3.0) & (y > g.rows - 1.0))
        | ((x == 1.0) & (col_place == 0))
        | ((x == g.cols + 2.0) & (col_place == 15))
    )
    return jnp.where(out, 0.0, 1.0)[0:1, :]


def block_kernel(strips, bias, *refs):
    wp_all, out = refs[:4], refs[4]
    xr_all, hr_all, z0, zt_all = refs[5:9], refs[9:13], refs[13], (None,) + refs[14:17]
    _, row_place, col_place = place()

    def body(g):
        c = g.channels
        cl = up128(c)
        xr, hr, wp = xr_all[g.b], hr_all[g.b], wp_all[g.b]

        def put(i, tile, source):
            lane, to, left = i * g.pitch, i * g.wide + tile * g.pitch, g.pitch
            while left:
                m, at = divmod(lane, 128)
                n = min(left, 128 - at)
                if 0 <= source < 4:
                    piece = strips[source, m * c : (m + 1) * c, at : at + n]
                else:
                    piece = jnp.zeros((c, n), BF)
                xr[c : 2 * c, to : to + n] = piece
                lane, to, left = lane + n, to + n, left - n

        for i in range(g.high):
            low = [k for k in range(4) if k * g.strip - 2 + i < 0]
            high = [k for k in range(4) if k * g.strip - 2 + i >= g.rows]
            for tile in range(4):
                put(i, tile, tile)
            if low:

                @pl.when(row_place <= max(low))
                def _(i=i):
                    for tile in range(4):
                        put(i, tile, tile - 1)

            if high:

                @pl.when(row_place >= min(high))
                def _(i=i):
                    for tile in range(4):
                        put(i, tile, tile + 1)

        mask = inside(g, row_place, col_place)

        def column(layer):
            wide = jnp.broadcast_to(bias[0, layer : layer + 1, :], (8, 8 * WIDTH))
            return wide.T[0:c, 0:1]

        def conv(layer, maps, size, n, finish):
            maps[0:c, 1:size] = maps[c : 2 * c, 0 : size - 1]
            maps[2 * c : 3 * c, 0 : size - 1] = maps[c : 2 * c, 1:size]
            thirds = [slice(0, 3 * c)]
            if g.b == 3:
                thirds = [slice(c * third, c * (third + 1)) for third in (1, 0, 2)]
            step = STEPS[g.b]
            for at in range(0, n, step):
                width = min(step, n - at)
                total = None
                for part in thirds:
                    for dy in range(3):
                        lane = at + dy * g.wide
                        term = nn(wp[layer, dy, :, part], maps[part, lane : lane + width])
                        total = term if total is None else total + term
                finish(at, width, total)

        bias0 = column(0)

        def finish_first(at, size, total):
            h = jnp.maximum(total + bias0, 0.0) * mask[:, at : at + size]
            hr[c : 2 * c, at : at + size] = h.astype(BF)

        conv(0, xr, g.lanes, g.n1, finish_first)

        bias1 = column(1)

        def finish_second(at, size, total):
            lane = 2 * g.wide + at
            z = jnp.maximum(total + bias1 + xr[c : 2 * c, lane : lane + size].astype(F32), 0.0)
            if g.b == 0:
                z0[:, at : at + size] = z.astype(BF)
            else:
                zt_all[g.b][at : at + size, :] = z.T

        conv(1, hr, g.n1, g.n2, finish_second)

        for tile in range(4):
            for i in range(g.strip):
                at = i * g.wide + tile * g.pitch + 2
                if g.b == 0:
                    out[tile, i * WIDTH : (i + 1) * WIDTH, :] = z0[:, at : at + g.cols]
                    continue
                values = zt_all[g.b][at : at + g.cols, :].astype(BF)
                for m in range(cl // 128):
                    r = (m * g.strip + i) * g.cols
                    lanes = min(128, c - 128 * m)
                    out[tile, r : r + g.cols, 0:lanes] = values[:, 128 * m : 128 * m + lanes]

    per_branch(body)


def repeat_map(j, i):
    gj, gi = GEO[j], GEO[i]
    shape = (gj.pixels // 4, gi.pixels // 4)
    fine = lax.broadcasted_iota(jnp.int32, shape, 0)
    coarse = lax.broadcasted_iota(jnp.int32, shape, 1)
    return cover(fine, coarse, gj, i - j)


def cover(fine, coarse, g, d):
    bits = 7 - g.b
    y = fine >> bits
    x = fine & (g.cols - 1)
    return (((y >> d) << (bits - d)) + (x >> d) == coarse).astype(F32).astype(BF)


def repeat_map_t(j, i):
    gj, gi = GEO[j], GEO[i]
    shape = (gi.pixels // 4, gj.pixels // 4)
    coarse = lax.broadcasted_iota(jnp.int32, shape, 0)
    fine = lax.broadcasted_iota(jnp.int32, shape, 1)
    return cover(fine, coarse, gj, i - j)


def nn(a, b):
    return jnp.dot(a, b, preferred_element_type=F32)


def nt(a, b):
    return lax.dot_general(a, b, (((1,), (1,)), ((), ())), preferred_element_type=F32)


def join_kernel(zb, weight, bias, out0, out1, out2, out3, z0s, s0):
    for y in range(8):
        z0s[:, 128 * y : 128 * (y + 1)] = zb[0, WIDTH * y : WIDTH * (y + 1), :]
    z = [
        z0s[...],
        zb[1, 0:256, 0:96],
        jnp.concatenate([zb[2, 0:64, :], zb[2, 64:128, 0:64]], axis=1),
        jnp.concatenate([zb[3, 0:16, :], zb[3, 16:32, :], zb[3, 32:48, :]], axis=1),
    ]

    def block(j, i, last=None):
        first, end = GEO[j], GEO[j if last is None else last]
        gi = GEO[i]
        rows = slice(first.start, end.start + end.channels)
        return weight[rows, gi.start : gi.start + gi.channels]

    def tn(a, b):
        return lax.dot_general(a, b, (((0,), (0,)), ((), ())), preferred_element_type=F32)

    size = [g.pixels // 4 for g in GEO]
    terms = {i: nt(z[i], block(0, i, i - 1)).astype(BF) for i in (1, 2, 3)}
    shrink0 = jnp.concatenate([repeat_map_t(0, i) for i in (1, 2, 3)], axis=0)
    shrink1 = jnp.concatenate([repeat_map_t(1, i) for i in (2, 3)], axis=0)
    sums = {0: nt(shrink0, z[0]), 1: nn(shrink1, z[1]), 2: nn(repeat_map_t(2, 3), z[2])}

    stacked = jnp.concatenate([terms[i][:, 0:WIDTH] for i in (1, 2, 3)], axis=0)
    wide = jnp.broadcast_to(bias[:, 0:WIDTH], (8, WIDTH))
    total = tn(stacked, shrink0) + z[0].astype(F32) + wide.T[:, 0:1]
    total = jnp.maximum(total, 0.0)
    for y in range(8):
        s0[:, y, :] = total[:, 128 * y : 128 * (y + 1)]
    out0[...] = s0[...].astype(BF)

    for j, out in ((1, out1), (2, out2), (3, out3)):
        g = GEO[j]
        total = z[j].astype(F32) + bias[:, g.start : g.start + g.channels]
        for i in range(j):
            first = sum(size[i + 1 : j])
            mean = (sums[i][first : first + size[j], :] * (0.25 ** (j - i))).astype(BF)
            total = total + nt(mean, block(j, i)).astype(BF).astype(F32)
        for i in range(j + 1, 4):
            term = terms[i][:, g.start : g.start + g.channels]
            total = total + nn(repeat_map(j, i), term)
        out[...] = jnp.maximum(total, 0.0).astype(BF)


def params(mib=24):
    return pltpu.CompilerParams(vmem_limit_bytes=mib * 1024 * 1024)


def like(*shapes):
    return tuple(jax.ShapeDtypeStruct(s, BF) for s in shapes)


def call_cols(x):
    return pl.pallas_call(
        cols_kernel,
        out_shape=like((WIDTH, 128), (WIDTH, 128), (WIDTH, TH * TW)),
        in_specs=[VMEM],
        out_specs=(VMEM,) * 3,
        scratch_shapes=[pltpu.VMEM((WIDTH, 128), BF)] * 2,
        compiler_params=params(),
    )(x)


def call_prepare(x, weight):
    shapes = [(g.channels, g.padded) for g in GEO]
    shapes += [(2, 3, g.channels, 3 * g.channels) for g in GEO]
    shapes += [(g.sides, g.padded) for g in GEO]
    shapes += [(g.channels, g.channels) for g in GEO[1:]]
    made = pl.pallas_call(
        prepare_kernel,
        out_shape=like(*shapes),
        in_specs=[VMEM, pl.BlockSpec(memory_space=pltpu.HBM)],
        out_specs=(VMEM,) * len(shapes),
        scratch_shapes=[pltpu.VMEM((g.channels, g.pixels), BF) for g in GEO[1:]]
        + [pltpu.VMEM((2, 3, 3, 192, 256), BF), pltpu.SemaphoreType.DMA((18,))],
        compiler_params=params(PREPARE_MIB),
        cost_estimate=pl.CostEstimate(flops=10**9, bytes_accessed=12 * 2**20, transcendentals=0),
    )(x, weight)
    return made[:4] + made[8:], made[4:8]


def call_strips(far, near, padded):
    scratch = [pltpu.VMEM((WIDTH, 128), BF)] * 2
    scratch += [pltpu.VMEM((g.channels, g.sides), BF) for g in GEO]
    scratch += [pltpu.VMEM((g.channels, g.padded), BF) for g in GEO]
    scratch += [pltpu.VMEM((g.channels, g.slot), BF) for g in GEO]
    return pl.pallas_call(
        strips_kernel,
        out_shape=like((4, SLOT_ROWS, 128))[0],
        in_specs=[VMEM] * (2 + len(padded)),
        out_specs=VMEM,
        scratch_shapes=scratch,
        compiler_params=params(),
    )(far, near, *padded)


def call_block(strips, bias, weights):
    scratch = [pltpu.VMEM((3 * g.channels, g.lanes), BF) for g in GEO]
    scratch += [pltpu.VMEM((3 * g.channels, g.n1), BF) for g in GEO]
    scratch += [pltpu.VMEM((WIDTH, GEO[0].n2), BF)]
    scratch += [pltpu.VMEM((g.n2, g.channels), F32) for g in GEO[1:]]
    return pl.pallas_call(
        block_kernel,
        out_shape=like((4, 384, 128))[0],
        in_specs=[VMEM] * 6,
        out_specs=VMEM,
        scratch_shapes=scratch,
        compiler_params=params(),
    )(strips, bias, *weights)


def call_join(received, weight, bias):
    return pl.pallas_call(
        join_kernel,
        out_shape=like((WIDTH, 8, 128), (256, 96), (64, 192), (16, 384)),
        in_specs=[VMEM] * 3,
        out_specs=(VMEM,) * 4,
        scratch_shapes=[
            pltpu.VMEM((WIDTH, 1024), BF),
            pltpu.VMEM((WIDTH, 8, 128), F32),
        ],
        compiler_params=params(),
    )(received, weight, bias)


def paired(shard, first):
    size = lax.axis_size("col")
    pairs = []
    for c in range(first, size - 1, 2):
        pairs += [(c, c + 1), (c + 1, c)]
    return lax.ppermute(shard, "col", pairs)


def swapped(parts, axis):
    return lax.all_to_all(parts, axis, split_axis=0, concat_axis=0, tiled=True)


def local(section_in, conv_weight, conv_bias, join_weight, join_bias):
    x = section_in[0, 0, 0]
    far, near, kept = call_cols(x)
    padded, weights = call_prepare(kept, conv_weight)
    strips = call_strips(paired(far, 1), paired(near, 0), padded)
    settled = call_block(swapped(strips, "row"), conv_bias, weights)
    out = call_join(swapped(settled, "branch"), join_weight, join_bias[None, :])
    first = [out[0]]
    for g in GEO[1:]:
        pixel_major = out[g.b].reshape(g.strip, g.cols, g.channels)
        first.append(pixel_major.transpose(2, 0, 1))
    return tuple(first)


def solution(mesh):
    in_specs = (
        P("branch", "row", "col", None, None),
        P("branch", None, None, None, None, None),
        P("branch", None, None),
        P(),
        P(),
    )
    out_specs = (P(None, ("branch", "row"), "col"),) * 4
    return jax.shard_map(local, mesh=mesh, in_specs=in_specs, out_specs=out_specs, check_vma=False)
```
